512 devices in a mesh: pre: 16 (over z), row: 32 (over x, y, core).
Axes of the slice: x: 4, y: 4, z: 16, core: 2. Of those that a mesh axis runs over, the one named last changes fastest.
Arguments:
- hidden_in: bfloat16 [4096, 8192], P('row'), may hold values from -6 to 6
- frozen_query_base: bfloat16 [4096, 1024], P('row'), may hold values from -10 to 10
- k_prefix: bfloat16 [32768, 128], P('pre'), may hold values from -6 to 6
- v_prefix: bfloat16 [32768, 128], P('pre'), may hold values from -6 to 6
- tree_mask: int32 [8, 256], P(None, 'pre'), may hold values from 0 to 1, as said below
- adapter_ids: int32 [8], replicated, may hold values from 0 to 7, each once
- a_down: bfloat16 [8192, 128], P('row'), may hold values from -0.0625 to 0.0625
- up_weight_matrix: bfloat16 [128, 1024], replicated, may hold values from -0.75 to 0.75
- cotangent: bfloat16 [4096, 1024], P('row'), may hold values from -6 to 6
Outputs:
- attended: bfloat16 [4096, 1024], P('row')
- grad_a: float32 [8192, 128], P('row')
- up_weight_gradient: float32 [128, 1024], replicated
The draws below stay inside these ranges and needn't reach their ends.
Inputs may be any that keep to these rules, and one draw needn't show every extreme that they name: `tree_mask`: every student reads mask block 0. The blocks that a student reads lie on one path of a tree of branches shared by the students: blocks near the start of the prefix are read by more students than blocks near its end.
All inputs are finite; a program needn't handle non-finite values.
Results may differ from the reference program's by a relative error of at most 0.014.
Values may be sent and summed in bfloat16 or wider, within the bound.
A program may use at most 64 MiB of HBM per device.

```python
import math
import jax
import jax.numpy as jnp
from jax import lax

D = 8192
HQ = 8
HD = 128
RANK = 16
S = 8
CONT = 512
MB = 128
PREFIX = 32768
TOKENS = 4096
NA = 8


def draw_k_prefix(key, part):
    base = jnp.clip(jax.random.normal(jax.random.fold_in(key, 1), (PREFIX, HD), jnp.float32), -6.0, 6.0)
    return base.astype(jnp.bfloat16)


def draw_frozen_query_base(key, part):
    base = jnp.clip(2.5 * jax.random.normal(jax.random.fold_in(key, 2), (TOKENS, HQ * HD), jnp.float32), -10.0, 10.0)
    return base.astype(jnp.bfloat16)


def draw_tree_mask(key, part):
    block_total = PREFIX // MB
    blocks = jnp.arange(block_total)
    bounds = [0, block_total // 4, block_total // 2, 3 * block_total // 4, block_total]
    reads = jnp.broadcast_to((blocks < bounds[1])[None, :], (S, block_total))
    for level in range(1, 4):
        branches = 2 ** level
        begin = bounds[level]
        finish = bounds[level + 1]
        span = finish - begin
        widths = jax.random.randint(jax.random.fold_in(key, 11 + level), (branches,), 1, 4)
        cuts = begin + jnp.cumsum(widths) * span // jnp.sum(widths)
        branch_of = jnp.sum((blocks[:, None] >= cuts[None, :-1]).astype(jnp.int32), axis=1)
        inside = (blocks >= begin) & (blocks < finish)
        student_branch = jnp.arange(S) * branches // S
        reads = reads | inside[None, :] & (branch_of[None, :] == student_branch[:, None])
    return reads.astype(jnp.int32)


def levels(own_key, extent, split, low, largest):
    gain, own = 1.0, jax.random.fold_in(own_key, 6)
    for position, parts in split:
        steps = jnp.exp(jax.random.uniform(jax.random.fold_in(own, position), (parts,), jnp.float32, low / len(split), largest / len(split)))
        gain = gain * jnp.repeat(steps, extent[position] // parts).reshape([-1 if axis == position else 1 for axis in range(len(extent))])
    return gain


def noise(key, extent, spread, reach, shards=(), held_as=jnp.bfloat16):
    values = jax.random.normal(key, extent, jnp.float32) * spread
    if len(shards) > 0:
        values = levels(key, extent, shards, -0.22, 0.18) * values
    return jnp.clip(values, min=-reach, max=reach).astype(held_as)


def setup_inputs(seed: int = 0) -> dict:
    splits = jax.random.split(jax.random.key(seed), 10)
    hidden_in = noise(splits[0], (TOKENS, D), 1.0, 6.0, ((0, 32),))
    frozen_query_base = draw_frozen_query_base(jax.random.fold_in(splits[9], 71), 0)
    k_prefix = draw_k_prefix(jax.random.fold_in(splits[9], 71), 0)
    v_prefix = noise(splits[3], (PREFIX, HD), 1.0, 6.0, ((0, 16),))
    tree_mask = draw_tree_mask(jax.random.fold_in(splits[9], 71), 0)
    adapter_ids = jax.random.permutation(splits[5], S).astype(jnp.int32)
    a_down = noise(splits[6], (D, NA * RANK), D ** -0.5, 0.0625, ((0, 32),))
    up_weight_matrix = noise(splits[7], (NA * RANK, HQ * HD), (4 * RANK) ** -0.5, 0.75)
    cotangent = noise(splits[8], (TOKENS, HQ * HD), 1.0, 6.0, ((0, 32),))
    return {"hidden_in": hidden_in, "frozen_query_base": frozen_query_base, "k_prefix": k_prefix, "v_prefix": v_prefix, "tree_mask": tree_mask, "adapter_ids": adapter_ids, "a_down": a_down, "up_weight_matrix": up_weight_matrix, "cotangent": cotangent}


ADAPTER_SCALE = 2.0

def reference(hidden_in, frozen_query_base, k_prefix, v_prefix, tree_mask, adapter_ids, a_down, up_weight_matrix, cotangent):
    score_scale = 1.0 / math.sqrt(HD)
    latent_full = jnp.dot(hidden_in, a_down, preferred_element_type=jnp.float32)
    student_of = (jnp.arange(TOKENS) // CONT).astype(jnp.int32)
    token_adapter = adapter_ids[student_of]
    column_mask = (jnp.arange(NA * RANK) // RANK)[None, :] == token_adapter[:, None]
    low_rank_code = jnp.where(column_mask, latent_full, jnp.float32(0.0)).astype(jnp.bfloat16)
    raised_query = jnp.dot(low_rank_code, up_weight_matrix, preferred_element_type=jnp.float32)
    student_queries = (frozen_query_base.astype(jnp.float32) + ADAPTER_SCALE * raised_query).astype(jnp.bfloat16)
    query_groups = student_queries.reshape(S, CONT, HQ, HD).transpose(0, 2, 1, 3).reshape(S * HQ, CONT, HD)
    upstream_groups = cotangent.reshape(S, CONT, HQ, HD).transpose(0, 2, 1, 3).reshape(S * HQ, CONT, HD)
    live_all = jnp.repeat(tree_mask > 0, MB, axis=1)
    group_student = (jnp.arange(S * HQ) // HQ).astype(jnp.int32)

    def per_group(inputs):
        query_rows, upstream, owner = inputs
        live_keys = live_all[owner][None, :]
        scores = jnp.dot(query_rows, k_prefix.T, preferred_element_type=jnp.float32) * score_scale
        row_max = lax.optimization_barrier(jnp.max(jnp.where(live_keys, scores, -jnp.inf), axis=1))
        expo = jnp.where(live_keys, jnp.exp(scores - row_max[:, None]), jnp.float32(0.0))
        row_sum = lax.optimization_barrier(jnp.sum(expo, axis=1))
        weights = expo.astype(jnp.bfloat16)
        summed = jnp.dot(weights, v_prefix, preferred_element_type=jnp.float32)
        attended_rows = (summed / row_sum[:, None]).astype(jnp.bfloat16)
        log_total = row_max + jnp.log(row_sum)
        probs = jnp.where(live_keys, jnp.exp(scores - log_total[:, None]), jnp.float32(0.0))
        row_delta = lax.optimization_barrier(jnp.sum(upstream.astype(jnp.float32) * attended_rows.astype(jnp.float32), axis=1))
        grad_probs = jnp.dot(upstream, v_prefix.T, preferred_element_type=jnp.float32)
        grad_scores = (probs * (grad_probs - row_delta[:, None])).astype(jnp.bfloat16)
        grad_rows = jnp.dot(grad_scores, k_prefix, preferred_element_type=jnp.float32) * score_scale
        return (attended_rows, grad_rows)
    attended_groups, grad_groups = lax.map(per_group, (query_groups, upstream_groups, group_student))
    attended = attended_groups.reshape(S, HQ, CONT, HD).transpose(0, 2, 1, 3).reshape(TOKENS, HQ * HD)
    query_gradient = grad_groups.reshape(S, HQ, CONT, HD).transpose(0, 2, 1, 3).reshape(TOKENS, HQ * HD).astype(jnp.bfloat16)
    backward_low_rank = ADAPTER_SCALE * jnp.dot(query_gradient, up_weight_matrix.T, preferred_element_type=jnp.float32)
    grad_latent = jnp.where(column_mask, backward_low_rank, jnp.float32(0.0)).astype(jnp.bfloat16)
    grad_a = jnp.dot(hidden_in.T, grad_latent, preferred_element_type=jnp.float32)
    up_weight_gradient = ADAPTER_SCALE * jnp.dot(low_rank_code.T, query_gradient, preferred_element_type=jnp.float32)
    return (attended, grad_a, up_weight_gradient)
```

```python
import functools
import math

import jax
import jax.numpy as jnp
from jax import lax
from jax.experimental import pallas as pl
from jax.experimental.pallas import tpu as pltpu
from jax.sharding import PartitionSpec as P

HD = 128
RANK = 16
MB = 128
ADAPTER_SCALE = 2.0
DEAD = -1e30
FLOOR = -1e29
TINY = 1e-30
SUBS = 2
MESH = pl.DeviceIdType.MESH
F32 = jnp.float32
BF16 = jnp.bfloat16


def dot(a, b, ca, cb):
    return lax.dot_general(a, b, (((ca,), (cb,)), ((), ())), preferred_element_type=F32)


def remote(src, dst, send_sem, recv_sem, pre, row):
    return pltpu.make_async_remote_copy(
        src_ref=src,
        dst_ref=dst,
        send_sem=send_sem,
        recv_sem=recv_sem,
        device_id=(pre, row),
        device_id_type=MESH,
    )


def picker(ids_ref, students, ranks):
    place = lax.broadcasted_iota(jnp.int32, (ranks, ranks), 0)
    column = lax.broadcasted_iota(jnp.int32, (ranks, ranks), 1)
    wanted = jnp.zeros((ranks, ranks), jnp.int32)
    for s in range(students):
        wanted = jnp.where(place // RANK == s, ids_ref[s] * RANK + place % RANK, wanted)
    return jnp.where(column == wanted, 1.0, 0.0).astype(BF16)


def query_kernel(
    per_student,
    row_count,
    ids_ref,
    a_ref,
    hidden_hbm,
    up_ref,
    base_ref,
    latent_ref,
    query_ref,
    own_up_ref,
    outgoing,
    incoming,
    hidden,
    send_sem,
    recv_sem,
    load_sem,
):
    pre = lax.axis_index("pre")
    row = lax.axis_index("row")
    students = row_count // per_student
    depth = a_ref.shape[0]
    ranks = a_ref.shape[1]
    barrier = pltpu.get_barrier_semaphore()

    def greet(k, carry):
        pl.semaphore_signal(
            barrier, inc=1, device_id=(pre, (row + k) % row_count), device_id_type=MESH
        )
        return carry

    lax.fori_loop(1, row_count, greet, 0)
    load = pltpu.make_async_copy(hidden_hbm, hidden, load_sem)
    load.start()
    pick = picker(ids_ref, students, ranks)
    picked = dot(pick, a_ref[...], 1, 1).astype(BF16)
    for s in range(students):
        outgoing[s] = picked[s * RANK : (s + 1) * RANK]
    pl.semaphore_wait(barrier, row_count - 1)

    def send(k, carry):
        to = (row + k) % row_count
        remote(
            outgoing.at[to // per_student],
            incoming.at[row],
            send_sem.at[k],
            recv_sem.at[row],
            pre,
            to,
        ).start()
        return carry

    lax.fori_loop(1, row_count, send, 0)
    load.wait()
    mine = row // per_student

    def project(k, total):
        source = (row - k + row_count) % row_count
        remote(
            outgoing.at[0], incoming.at[source], send_sem.at[0], recv_sem.at[source], pre, row
        ).wait_recv()
        block = hidden[:, pl.ds(pl.multiple_of(source * depth, depth), depth)]
        return total + dot(incoming[source], block, 1, 1)

    own = dot(outgoing[mine], hidden[:, pl.ds(pl.multiple_of(row * depth, depth), depth)], 1, 1)
    total = lax.fori_loop(1, row_count, project, own)
    latent = total.astype(BF16)
    latent_ref[...] = latent
    place = lax.broadcasted_iota(jnp.int32, (RANK, ranks), 0)
    column = lax.broadcasted_iota(jnp.int32, (RANK, ranks), 1)
    own_pick = jnp.where(column == ids_ref[mine] * RANK + place, 1.0, 0.0).astype(BF16)
    up = dot(own_pick, up_ref[...], 1, 0).astype(BF16)
    own_up_ref[...] = up
    raised = dot(latent, up, 0, 0)
    query_ref[...] = (base_ref[...].astype(F32) + ADAPTER_SCALE * raised).astype(BF16)

    def finish(k, carry):
        remote(
            outgoing.at[0], incoming.at[0], send_sem.at[k], recv_sem.at[0], pre, row
        ).wait_send()
        return carry

    lax.fori_loop(1, row_count, finish, 0)


def split_parts(x, count):
    parts = []
    for _ in range(count):
        part = x.astype(BF16).astype(F32)
        parts.append(part)
        x = x - part
    return parts


def merge(first, second, fold):
    m1, l1, d1, o1, b1, a1 = first
    m2, l2, d2, o2, b2, a2 = second
    m = jnp.maximum(m1, m2)
    f1 = jnp.exp2((m1 - m) * fold)
    f2 = jnp.exp2((m2 - m) * fold)
    w1 = f1 * l1
    w2 = f2 * l2
    total = w1 + w2
    centre = (w1 * d1 + w2 * d2) / jnp.maximum(total, TINY)
    o = f1 * o1 + f2 * o2
    b = f1 * b1 + f2 * b2
    a = f1 * (a1 + (d1 - centre) * b1) + f2 * (a2 + (d2 - centre) * b2)
    return (m, total, centre, o, b, a)


def attention_kernel(
    pre_count,
    row_count,
    per_student,
    ids_ref,
    mask_ref,
    query_ref,
    upstream_ref,
    key_ref,
    value_ref,
    latent_ref,
    up_ref,
    hidden_hbm,
    attended_ref,
    grad_a_ref,
    grad_up_ref,
    hidden,
    q_rows,
    u_rows,
    bias,
    value_key,
    scores,
    local,
    ring_out,
    ring_in,
    fixed,
    term_out,
    term_in,
    att_out,
    att_in,
    quarter_out,
    quarter_in,
    grad_out,
    grad_in,
    up_out,
    up_in,
    raised,
    grad_rows,
    up_rows,
    load_sem,
    ring_send,
    ring_recv,
    term_send,
    term_recv,
    att_send,
    att_recv,
    quarter_send,
    quarter_recv,
    grad_send,
    grad_recv,
    up_send,
    up_recv,
):
    pre = lax.axis_index("pre")
    row = lax.axis_index("row")
    tokens = query_ref.shape[0]
    heads = query_ref.shape[1] // HD
    keys = key_ref.shape[0]
    students = row_count // per_student
    own_rows = heads * tokens // pre_count
    pieces = tokens // own_rows
    sub_rows = own_rows // SUBS
    half = pre_count // 2
    score_scale = 1.0 / math.sqrt(HD)
    fold = score_scale * math.log2(math.e)
    student = row // per_student
    place = row % per_student
    first_row = student * per_student
    depth = grad_a_ref.shape[0]
    width = grad_up_ref.shape[1] // per_student
    barrier = pltpu.get_barrier_semaphore()

    def greet_row(k, carry):
        pl.semaphore_signal(
            barrier, inc=1, device_id=(pre, (row + k) % row_count), device_id_type=MESH
        )
        return carry

    def greet_pre(k, carry):
        pl.semaphore_signal(
            barrier, inc=1, device_id=((pre + k) % pre_count, row), device_id_type=MESH
        )
        return carry

    lax.fori_loop(1, pre_count, greet_pre, 0)
    lax.fori_loop(1, row_count, greet_row, 0)
    load = pltpu.make_async_copy(hidden_hbm, hidden, load_sem)
    load.start()

    value_key[:, :HD] = value_ref[...]
    value_key[:, HD:] = key_ref[...]
    for h in range(heads):
        q_rows[h * tokens : (h + 1) * tokens, :] = query_ref[:, h * HD : (h + 1) * HD]
        u_rows[h * tokens : (h + 1) * tokens, :] = upstream_ref[:, h * HD : (h + 1) * HD]
    for b in range(keys // MB):
        read = jnp.full((8, MB), mask_ref[student, b], jnp.int32)
        bias[:, b * MB : (b + 1) * MB] = jnp.where(read > 0, 0.0, DEAD)
    block = min(256, heads * tokens)
    step = min(512, keys)

    def attend(i, carry):
        rows = pl.ds(pl.multiple_of(i * block, block), block)
        q = q_rows[rows, :]
        u = u_rows[rows, :]
        high = jnp.full((block, HD), FLOOR, F32)
        for j in range(keys // step):
            cols = slice(j * step, (j + 1) * step)
            s = dot(q, key_ref[cols, :], 1, 1) + bias[0:1, cols]
            scores[:, cols] = s
            for g in range(step // HD):
                high = jnp.maximum(high, s[:, g * HD : (g + 1) * HD])
        m = jnp.max(high, axis=1, keepdims=True)
        sums = jnp.zeros((block, HD), F32)
        both = jnp.zeros((block, 2 * HD), F32)
        for j in range(keys // step):
            cols = slice(j * step, (j + 1) * step)
            w = jnp.exp2((scores[:, cols] - m) * fold)
            scores[:, cols] = w
            for g in range(step // HD):
                sums = sums + w[:, g * HD : (g + 1) * HD]
            both = both + dot(w.astype(BF16), value_key[cols, :], 1, 0)
        l = jnp.sum(sums, axis=1, keepdims=True)
        o = both[:, :HD]
        d = jnp.sum(u.astype(F32) * o, axis=1, keepdims=True) / jnp.maximum(l, TINY)
        a = jnp.zeros((block, HD), F32)
        for j in range(keys // step):
            cols = slice(j * step, (j + 1) * step)
            dp = dot(u, value_ref[cols, :], 1, 1)
            g = (scores[:, cols] * (dp - d)).astype(BF16)
            a = a + dot(g, key_ref[cols, :], 1, 0)
        local[0, rows, :] = jnp.broadcast_to(m, (block, HD))
        local[1, rows, :] = jnp.broadcast_to(l, (block, HD))
        local[2, rows, :] = jnp.broadcast_to(d, (block, HD))
        local[3, rows, :] = o
        local[4, rows, :] = both[:, HD:]
        local[5, rows, :] = a
        return carry

    lax.fori_loop(0, heads * tokens // block, attend, 0)

    lane_in = lax.broadcasted_iota(jnp.int32, (HD, 3 * HD), 0)
    lane_out = lax.broadcasted_iota(jnp.int32, (HD, 3 * HD), 1) // HD
    spread = jnp.where(
        (lane_in < 3) & (lane_out == 0)
        | (lane_in >= 3) & (lane_in < 5) & (lane_out == 1)
        | (lane_in >= 5) & (lane_in < 7) & (lane_out == 2),
        1.0,
        0.0,
    ).astype(BF16)
    fixed[...] = spread
    lane = lax.broadcasted_iota(jnp.int32, (sub_rows, HD), 1)

    def local_term(chunk, sub):
        rows = pl.ds(pl.multiple_of(chunk * own_rows + sub * sub_rows, sub_rows), sub_rows)
        return tuple(local[n, rows, :] for n in range(6))

    def arrived(flow, t, sub):
        data = ring_in[flow, t, sub]
        stats = dot(data[:, 3 * HD :], fixed[...], 1, 0)
        return (
            stats[:, :HD],
            stats[:, HD : 2 * HD],
            stats[:, 2 * HD :],
            data[:, :HD].astype(F32),
            data[:, HD : 2 * HD].astype(F32),
            data[:, 2 * HD : 3 * HD].astype(F32),
        )

    def ring_copy(flow, t, sub):
        step_to = 1 if flow == 0 else pre_count - 1
        return remote(
            ring_out.at[flow, t, sub],
            ring_in.at[flow, t, sub],
            ring_send.at[flow, t, sub],
            ring_recv.at[flow, t, sub],
            (pre + step_to) % pre_count,
            row,
        )

    def pass_on(flow, t, sub, term):
        m, l, d, o, b, a = term
        parts = split_parts(m, 3) + split_parts(l, 2) + split_parts(d, 2)
        stats = jnp.zeros((sub_rows, HD), F32)
        for n, part in enumerate(parts):
            stats = jnp.where(lane == n, part, stats)
        ring_out[flow, t, sub, :, :HD] = o.astype(BF16)
        ring_out[flow, t, sub, :, HD : 2 * HD] = b.astype(BF16)
        ring_out[flow, t, sub, :, 2 * HD : 3 * HD] = a.astype(BF16)
        ring_out[flow, t, sub, :, 3 * HD :] = stats.astype(BF16)
        ring_copy(flow, t, sub).start()

    def chunk_of(flow, t):
        if flow == 0:
            return (pre + half - t) % pre_count
        return (pre + half + t) % pre_count

    pl.semaphore_wait(barrier, row_count - 1 + pre_count - 1)
    for sub in range(SUBS):
        pass_on(1, 0, sub, local_term(chunk_of(1, 0), sub))
    for sub in range(SUBS):
        pass_on(0, 1, sub, local_term(chunk_of(0, 1), sub))
    for sub in range(SUBS):
        ring_copy(1, 0, sub).wait_recv()
        pass_on(1, 1, sub, merge(arrived(1, 0, sub), local_term(chunk_of(1, 1), sub), fold))

    def ring_step(t, carry):
        for sub in range(SUBS):
            for flow in (0, 1):
                ring_copy(flow, t - 1, sub).wait_recv()
                term = merge(arrived(flow, t - 1, sub), local_term(chunk_of(flow, t), sub), fold)
                pass_on(flow, t, sub, term)
        return carry

    lax.fori_loop(2, half, ring_step, 0)

    head = pre // pieces
    piece = pre % pieces
    parts = []
    for sub in range(SUBS):
        ring_copy(0, half - 1, sub).wait_recv()
        term = merge(arrived(0, half - 1, sub), local_term(pre, sub), fold)
        ring_copy(1, half - 1, sub).wait_recv()
        m, l, d, o, b, a = merge(term, arrived(1, half - 1, sub), fold)
        inverse = 1.0 / l
        attended = (o * inverse).astype(BF16)
        rows = pl.ds(pl.multiple_of(pre * own_rows + sub * sub_rows, sub_rows), sub_rows)
        u = u_rows[rows, :].astype(F32)
        delta = jnp.sum(u * attended.astype(F32), axis=1, keepdims=True)
        att_out[sub * sub_rows : (sub + 1) * sub_rows, :] = attended
        parts.append((((a + (d - delta) * b) * inverse) * score_scale).astype(BF16))
    grad_q = jnp.concatenate(parts * pieces, axis=0)
    piece_of = lax.broadcasted_iota(jnp.int32, (tokens, HD), 0) // own_rows
    grad_q = jnp.where(piece_of == piece, grad_q.astype(F32), 0.0).astype(BF16)
    up_head = up_ref[:, pl.ds(pl.multiple_of(head * HD, HD), HD)]
    term_out[:RANK, :tokens] = (ADAPTER_SCALE * dot(up_head, grad_q, 1, 1)).astype(BF16)
    term_out[RANK:, :HD] = (ADAPTER_SCALE * dot(latent_ref[...], grad_q, 1, 0)).astype(BF16)

    def term_copy(k):
        to = (pre + k) % pre_count
        return remote(term_out, term_in.at[pre], term_send.at[k], term_recv.at[pre], to, row)

    def att_copy(k):
        to = (pre + k) % pre_count
        return remote(att_out, att_in.at[pre], att_send.at[k], att_recv.at[pre], to, row)

    def send_term(k, carry):
        term_copy((k + half - 1) % (pre_count - 1) + 1).start()
        return carry

    def send_att(k, carry):
        att_copy((k + half - 1) % (pre_count - 1) + 1).start()
        return carry

    lax.fori_loop(0, pre_count - 1, send_term, 0)
    lax.fori_loop(0, pre_count - 1, send_att, 0)
    term_in[pre] = term_out[...]
    att_in[pre] = att_out[...]

    def take_term(k, carry):
        source = (pre + k) % pre_count
        remote(
            term_out, term_in.at[source], term_send.at[0], term_recv.at[source], pre, row
        ).wait_recv()
        return carry

    load.wait()
    lax.fori_loop(1, pre_count, take_term, 0)
    code = jnp.zeros((RANK, tokens), F32)
    for h in range(heads):
        lifted = jnp.zeros((RANK, HD), F32)
        for n in range(pieces):
            code = code + term_in[h * pieces + n, :RANK, :tokens].astype(F32)
            lifted = lifted + term_in[h * pieces + n, RANK:, :HD].astype(F32)
        raised[:, h * HD : (h + 1) * HD] = lifted
    for n in range(per_student):
        quarter_out[n] = raised[:, n * width : (n + 1) * width].astype(BF16)

    def quarter_copy(k):
        to = (place + k) % per_student
        return remote(
            quarter_out.at[to],
            quarter_in.at[place],
            quarter_send.at[k],
            quarter_recv.at[place],
            pre,
            first_row + to,
        )

    for k in range(1, per_student):
        quarter_copy(k).start()
    code = code.astype(BF16)

    def grad_copy(k, to):
        return remote(
            grad_out.at[to], grad_in.at[row], grad_send.at[k], grad_recv.at[row], pre, to
        )

    def send_grad(k, carry):
        to = (row + k) % row_count
        cols = pl.ds(pl.multiple_of(to * depth, depth), depth)
        grad_out[to] = dot(code, hidden[:, cols], 1, 0).astype(BF16)
        grad_copy(k, to).start()
        return carry

    lax.fori_loop(1, row_count, send_grad, 0)
    cols = pl.ds(pl.multiple_of(row * depth, depth), depth)
    grad_in[row] = dot(code, hidden[:, cols], 1, 0).astype(BF16)

    quarter_in[place] = quarter_out[place]
    for k in range(1, per_student):
        source = (place + k) % per_student
        remote(
            quarter_out.at[0],
            quarter_in.at[source],
            quarter_send.at[0],
            quarter_recv.at[source],
            pre,
            row,
        ).wait_recv()
    summed = jnp.zeros((RANK, width), F32)
    for n in range(per_student):
        summed = summed + quarter_in[n].astype(F32)
    up_out[...] = summed.astype(BF16)

    def up_copy(k):
        to = (row + k) % row_count
        return remote(up_out, up_in.at[row], up_send.at[k], up_recv.at[row], pre, to)

    def send_up(k, carry):
        up_copy(k).start()
        return carry

    lax.fori_loop(1, row_count, send_up, 0)
    up_in[row] = up_out[...]

    pick = picker(ids_ref, students, students * RANK)

    def take_grad(k, carry):
        source = (row + k) % row_count
        remote(
            grad_out.at[0], grad_in.at[source], grad_send.at[0], grad_recv.at[source], pre, row
        ).wait_recv()
        return carry

    lax.fori_loop(1, row_count, take_grad, 0)
    for s in range(students):
        block_sum = grad_in[s * per_student].astype(F32)
        for n in range(1, per_student):
            block_sum = block_sum + grad_in[s * per_student + n].astype(F32)
        for n, part in enumerate(split_parts(block_sum, 2)):
            grad_rows[n, s * RANK : (s + 1) * RANK, :] = part.astype(BF16)
    grad_a_ref[...] = dot(grad_rows[0], pick, 0, 0) + dot(grad_rows[1], pick, 0, 0)

    def take_up(k, carry):
        source = (row + k) % row_count
        remote(
            up_out, up_in.at[source], up_send.at[0], up_recv.at[source], pre, row
        ).wait_recv()
        return carry

    lax.fori_loop(1, row_count, take_up, 0)
    for s in range(students):
        for j in range(per_student):
            up_rows[s * RANK : (s + 1) * RANK, j * width : (j + 1) * width] = up_in[
                s * per_student + j
            ]
    grad_up_ref[...] = dot(pick, up_rows[...], 0, 0)

    def take_att(k, carry):
        source = (pre + k) % pre_count
        remote(
            att_out, att_in.at[source], att_send.at[0], att_recv.at[source], pre, row
        ).wait_recv()
        return carry

    lax.fori_loop(1, pre_count, take_att, 0)
    for h in range(heads):
        for n in range(pieces):
            attended_ref[
                n * own_rows : (n + 1) * own_rows, h * HD : (h + 1) * HD
            ] = att_in[h * pieces + n]

    for sub in range(SUBS):
        ring_copy(1, 0, sub).wait_send()

    def ring_done(t, carry):
        for sub in range(SUBS):
            for flow in (0, 1):
                ring_copy(flow, t, sub).wait_send()
        return carry

    lax.fori_loop(1, half, ring_done, 0)

    def pre_done(k, carry):
        term_copy(k).wait_send()
        att_copy(k).wait_send()
        return carry

    lax.fori_loop(1, pre_count, pre_done, 0)
    for k in range(1, per_student):
        quarter_copy(k).wait_send()

    def row_done(k, carry):
        grad_copy(k, (row + k) % row_count).wait_send()
        up_copy(k).wait_send()
        return carry

    lax.fori_loop(1, row_count, row_done, 0)


def vmem():
    return pl.BlockSpec(memory_space=pltpu.VMEM)


def smem():
    return pl.BlockSpec(memory_space=pltpu.SMEM)


def anywhere():
    return pl.BlockSpec(memory_space=pl.ANY)


def shards(
    pre_count,
    row_count,
    hidden_in,
    frozen_query_base,
    k_prefix,
    v_prefix,
    tree_mask,
    adapter_ids,
    a_down,
    up_weight_matrix,
    cotangent,
):
    tokens, width = frozen_query_base.shape
    model = hidden_in.shape[1]
    heads = width // HD
    keys = k_prefix.shape[0]
    depth, ranks = a_down.shape
    students = tree_mask.shape[0]
    per_student = row_count // students
    dma = pltpu.SemaphoreType.DMA
    latent, queries, own_up = pl.pallas_call(
        functools.partial(query_kernel, per_student, row_count),
        out_shape=(
            jax.ShapeDtypeStruct((RANK, tokens), BF16),
            jax.ShapeDtypeStruct((tokens, width), BF16),
            jax.ShapeDtypeStruct((RANK, width), BF16),
        ),
        in_specs=[smem(), vmem(), anywhere(), vmem(), vmem()],
        out_specs=(vmem(), vmem(), vmem()),
        scratch_shapes=[
            pltpu.VMEM((students, RANK, depth), BF16),
            pltpu.VMEM((row_count, RANK, depth), BF16),
            pltpu.VMEM((tokens, model), BF16),
            dma((row_count,)),
            dma((row_count,)),
            dma,
        ],
        compiler_params=pltpu.CompilerParams(collective_id=0, has_side_effects=True),
        name="queries",
    )(adapter_ids, a_down, hidden_in, up_weight_matrix, frozen_query_base)

    rows = heads * tokens
    own_rows = rows // pre_count
    half = pre_count // 2
    quarter = width // per_student
    attended, grad_a, grad_up = pl.pallas_call(
        functools.partial(attention_kernel, pre_count, row_count, per_student),
        out_shape=(
            jax.ShapeDtypeStruct((tokens, width), BF16),
            jax.ShapeDtypeStruct((depth, ranks), F32),
            jax.ShapeDtypeStruct((ranks, width), F32),
        ),
        in_specs=[smem(), smem()] + [vmem()] * 6 + [anywhere()],
        out_specs=(vmem(), vmem(), vmem()),
        scratch_shapes=[
            pltpu.VMEM((tokens, model), BF16),
            pltpu.VMEM((rows, HD), BF16),
            pltpu.VMEM((rows, HD), BF16),
            pltpu.VMEM((8, keys), F32),
            pltpu.VMEM((keys, 2 * HD), BF16),
            pltpu.VMEM((min(256, rows), keys), F32),
            pltpu.VMEM((6, rows, HD), F32),
            pltpu.VMEM((2, half, SUBS, own_rows // SUBS, 4 * HD), BF16),
            pltpu.VMEM((2, half, SUBS, own_rows // SUBS, 4 * HD), BF16),
            pltpu.VMEM((HD, 3 * HD), BF16),
            pltpu.VMEM((2 * RANK, HD), BF16),
            pltpu.VMEM((pre_count, 2 * RANK, HD), BF16),
            pltpu.VMEM((own_rows, HD), BF16),
            pltpu.VMEM((pre_count, own_rows, HD), BF16),
            pltpu.VMEM((per_student, RANK, quarter), BF16),
            pltpu.VMEM((per_student, RANK, quarter), BF16),
            pltpu.VMEM((row_count, RANK, depth), BF16),
            pltpu.VMEM((row_count, RANK, depth), BF16),
            pltpu.VMEM((RANK, quarter), BF16),
            pltpu.VMEM((row_count, RANK, quarter), BF16),
            pltpu.VMEM((RANK, width), F32),
            pltpu.VMEM((2, ranks, depth), BF16),
            pltpu.VMEM((ranks, width), BF16),
            dma,
            dma((2, half, SUBS)),
            dma((2, half, SUBS)),
            dma((pre_count,)),
            dma((pre_count,)),
            dma((pre_count,)),
            dma((pre_count,)),
            dma((per_student,)),
            dma((per_student,)),
            dma((row_count,)),
            dma((row_count,)),
            dma((row_count,)),
            dma((row_count,)),
        ],
        compiler_params=pltpu.CompilerParams(collective_id=1, has_side_effects=True),
        name="attention",
    )(
        adapter_ids,
        tree_mask,
        queries,
        cotangent,
        k_prefix,
        v_prefix,
        latent,
        own_up,
        hidden_in,
    )
    return (attended, grad_a, grad_up)


def solution(mesh):
    in_specs = (
        P("row", None),
        P("row", None),
        P("pre", None),
        P("pre", None),
        P(None, "pre"),
        P(),
        P("row", None),
        P(),
        P("row", None),
    )
    out_specs = (P("row", None), P("row", None), P())
    body = functools.partial(shards, mesh.shape["pre"], mesh.shape["row"])
    return jax.shard_map(body, mesh=mesh, in_specs=in_specs, out_specs=out_specs, check_vma=False)
```

```python
import functools
import math

import jax
import jax.numpy as jnp
from jax import lax
from jax.experimental import pallas as pl
from jax.experimental.pallas import tpu as pltpu
from jax.sharding import PartitionSpec as P

HD = 128
RANK = 16
MB = 128
ADAPTER_SCALE = 2.0
DEAD = -1e30
FLOOR = -1e29
TINY = 1e-30
BLOCK = 512
LOG2E = math.log2(math.e)
MESH = pl.DeviceIdType.MESH
F32 = jnp.float32
BF16 = jnp.bfloat16


def dot(a, b, ca, cb):
    return lax.dot_general(a, b, (((ca,), (cb,)), ((), ())), preferred_element_type=F32)


def remote(src, dst, send_sem, recv_sem, pre, row):
    return pltpu.make_async_remote_copy(
        src_ref=src,
        dst_ref=dst,
        send_sem=send_sem,
        recv_sem=recv_sem,
        device_id=(pre, row),
        device_id_type=MESH,
    )


def plane_offsets(row_count):
    extent = (4, 4, 2) if row_count == 32 else (1, row_count // 2, 2)
    around = lambda n, size: min(n, size - n)
    offsets = [
        (around(x, extent[0]) + around(y, extent[1]), x, y, c)
        for x in range(extent[0])
        for y in range(extent[1])
        for c in range(extent[2])
    ]
    return extent, [o[1:] for o in sorted(offsets, key=lambda o: -o[0]) if o[1:] != (0, 0, 0)]


def plane_peer(row, extent, offset):
    _, ys, cs = extent
    x = (row // (ys * cs) + offset[0]) % extent[0]
    y = (row // cs % ys + offset[1]) % ys
    return (x * ys + y) * cs + (row % cs + offset[2]) % cs


def line_offsets(count):
    return sorted(range(1, count), key=lambda k: -min(k, count - k))


def picker(ids_ref, students, ranks):
    place = lax.broadcasted_iota(jnp.int32, (ranks, ranks), 0)
    column = lax.broadcasted_iota(jnp.int32, (ranks, ranks), 1)
    wanted = jnp.zeros((ranks, ranks), jnp.int32)
    for s in range(students):
        wanted = jnp.where(place // RANK == s, ids_ref[s] * RANK + place % RANK, wanted)
    return jnp.where(column == wanted, 1.0, 0.0).astype(BF16)


def query_kernel(
    per_student,
    row_count,
    ids_ref,
    a_ref,
    hidden_hbm,
    up_ref,
    base_ref,
    latent_ref,
    query_ref,
    own_up_ref,
    outgoing,
    incoming,
    hidden,
    send_sem,
    recv_sem,
    load_sem,
):
    pre = lax.axis_index("pre")
    row = lax.axis_index("row")
    students = row_count // per_student
    depth = a_ref.shape[0]
    ranks = a_ref.shape[1]
    barrier = pltpu.get_barrier_semaphore()

    def greet(k, carry):
        pl.semaphore_signal(
            barrier, inc=1, device_id=(pre, (row + k) % row_count), device_id_type=MESH
        )
        return carry

    lax.fori_loop(1, row_count, greet, 0)
    load = pltpu.make_async_copy(hidden_hbm, hidden, load_sem)
    load.start()
    pick = picker(ids_ref, students, ranks)
    picked = dot(pick, a_ref[...], 1, 1).astype(BF16)
    for s in range(students):
        outgoing[s] = picked[s * RANK : (s + 1) * RANK]
    pl.semaphore_wait(barrier, row_count - 1)

    extent, offsets = plane_offsets(row_count)
    copies = []
    for k, offset in enumerate(offsets):
        to = plane_peer(row, extent, offset)
        copies.append(
            remote(
                outgoing.at[to // per_student],
                incoming.at[row],
                send_sem.at[k],
                recv_sem.at[row],
                pre,
                to,
            )
        )
        copies[-1].start()
    load.wait()
    mine = row // per_student

    def project(k, total):
        source = (row - k + row_count) % row_count
        remote(
            outgoing.at[0], incoming.at[source], send_sem.at[0], recv_sem.at[source], pre, row
        ).wait_recv()
        block = hidden[:, pl.ds(pl.multiple_of(source * depth, depth), depth)]
        return total + dot(incoming[source], block, 1, 1)

    own = dot(outgoing[mine], hidden[:, pl.ds(pl.multiple_of(row * depth, depth), depth)], 1, 1)
    total = lax.fori_loop(1, row_count, project, own)
    latent = total.astype(BF16)
    latent_ref[...] = latent
    place = lax.broadcasted_iota(jnp.int32, (RANK, ranks), 0)
    column = lax.broadcasted_iota(jnp.int32, (RANK, ranks), 1)
    own_pick = jnp.where(column == ids_ref[mine] * RANK + place, 1.0, 0.0).astype(BF16)
    up = dot(own_pick, up_ref[...], 1, 0).astype(BF16)
    own_up_ref[...] = up
    raised = dot(latent, up, 0, 0)
    query_ref[...] = (base_ref[...].astype(F32) + ADAPTER_SCALE * raised).astype(BF16)

    for copy in copies:
        copy.wait_send()


def split_parts(x, count):
    parts = []
    for _ in range(count):
        part = x.astype(BF16).astype(F32)
        parts.append(part)
        x = x - part
    return parts


def attention_kernel(
    pre_count,
    row_count,
    per_student,
    mask_ref,
    query_ref,
    upstream_ref,
    key_ref,
    value_ref,
    latent_ref,
    up_ref,
    hidden_hbm,
    attended_ref,
    grad_ref,
    raised_ref,
    hidden,
    q_rows,
    u_rows,
    bias,
    value_key,
    weights,
    high_rows,
    delta_rows,
    local,
    part,
    stat,
    stat_out,
    stat_in,
    chain_out,
    chain_in,
    odd_out,
    odd_in,
    term_out,
    term_in,
    att_in,
    quarter_out,
    quarter_in,
    grad_out,
    grad_in,
    up_out,
    up_in,
    raised,
    load_sem,
    stat_send,
    stat_recv,
    chain_send,
    chain_recv,
    odd_send,
    odd_recv,
    term_send,
    term_recv,
    att_send,
    att_recv,
    quarter_send,
    quarter_recv,
    grad_send,
    grad_recv,
    up_send,
    up_recv,
):
    pre = lax.axis_index("pre")
    row = lax.axis_index("row")
    tokens = query_ref.shape[0]
    heads = query_ref.shape[1] // HD
    keys = key_ref.shape[0]
    own_rows = heads * tokens // pre_count
    pieces = tokens // own_rows
    half = pre_count // 2
    steps = half // 2
    score_scale = 1.0 / math.sqrt(HD)
    fold = score_scale * LOG2E
    student = row // per_student
    place = row % per_student
    first_row = student * per_student
    depth = grad_out.shape[2]
    width = heads * HD // per_student
    extent, plane = plane_offsets(row_count)
    line = line_offsets(pre_count)
    barrier = pltpu.get_barrier_semaphore()

    for k in line:
        pl.semaphore_signal(
            barrier, inc=1, device_id=((pre + k) % pre_count, row), device_id_type=MESH
        )
    for offset in plane:
        pl.semaphore_signal(
            barrier, inc=1, device_id=(pre, plane_peer(row, extent, offset)), device_id_type=MESH
        )
    load = pltpu.make_async_copy(hidden_hbm, hidden, load_sem)
    load.start()

    value_key[:, :HD] = value_ref[...]
    value_key[:, HD:] = key_ref[...]
    for h in range(heads):
        q_rows[h * tokens : (h + 1) * tokens, :] = query_ref[:, h * HD : (h + 1) * HD]
        u_rows[h * tokens : (h + 1) * tokens, :] = upstream_ref[:, h * HD : (h + 1) * HD]
    for b in range(keys // MB):
        read = jnp.full((8, MB), mask_ref[student, b], jnp.int32)
        bias[:, b * MB : (b + 1) * MB] = jnp.where(read > 0, 0.0, DEAD)
    block = min(BLOCK, heads * tokens)
    step = min(512, keys)
    lane = lax.broadcasted_iota(jnp.int32, (tokens, HD), 1)
    stat[...] = jnp.zeros((tokens, HD), F32)

    def forward(i, carry):
        rows = pl.ds(pl.multiple_of(i * block, block), block)
        q = q_rows[rows, :]
        high = jnp.full((block, HD), FLOOR, F32)
        for j in range(keys // step):
            cols = slice(j * step, (j + 1) * step)
            s = dot(q, key_ref[cols, :], 1, 1) + bias[0:1, cols]
            weights[rows, cols] = s
            for g in range(step // HD):
                high = jnp.maximum(high, s[:, g * HD : (g + 1) * HD])
        m = jnp.max(high, axis=1, keepdims=True)
        sums = jnp.zeros((block, HD), F32)
        both = jnp.zeros((block, 2 * HD), F32)
        for j in range(keys // step):
            cols = slice(j * step, (j + 1) * step)
            w = jnp.exp2((weights[rows, cols] - m) * fold)
            weights[rows, cols] = w
            for g in range(step // HD):
                sums = sums + w[:, g * HD : (g + 1) * HD]
            both = both + dot(w.astype(BF16), value_key[cols, :], 1, 0)
        l = jnp.maximum(jnp.sum(sums, axis=1, keepdims=True), TINY)
        o = both[:, :HD]
        d = jnp.sum(u_rows[rows, :].astype(F32) * o, axis=1, keepdims=True) / l
        lse = m * fold + jnp.log(l) * LOG2E
        high_rows[rows, :] = jnp.broadcast_to(m * fold, (block, HD))
        delta_rows[rows, :] = jnp.broadcast_to(d, (block, HD))
        local[0, rows, :] = o
        local[1, rows, :] = both[:, HD:]
        table = stat[...]
        for n in range(block // tokens):
            h = i * (block // tokens) + n
            piece_rows = slice(n * tokens, (n + 1) * tokens)
            table = jnp.where(lane == h, lse[piece_rows], table)
            table = jnp.where(lane == heads + h, d[piece_rows], table)
        stat[...] = table
        return carry

    lax.fori_loop(0, heads * tokens // block, forward, 0)

    stat_out[...] = stat[...].T[: 2 * heads]
    stat_in[pre] = stat_out[...]
    pl.semaphore_wait(barrier, row_count - 1 + pre_count - 1)

    def line_copies(source, landing, send_sem, recv_sem):
        return [
            remote(
                source,
                landing.at[pre],
                send_sem.at[n],
                recv_sem.at[pre],
                (pre + k) % pre_count,
                row,
            )
            for n, k in enumerate(line)
        ]

    def take_line(source, landing, send_sem, recv_sem):
        for k in reversed(line):
            origin = (pre + k) % pre_count
            remote(
                source, landing.at[origin], send_sem.at[0], recv_sem.at[origin], pre, row
            ).wait_recv()

    stat_copies = line_copies(stat_out, stat_in, stat_send, stat_recv)
    for copy in stat_copies:
        copy.start()

    def backward(i, carry):
        rows = pl.ds(pl.multiple_of(i * block, block), block)
        u = u_rows[rows, :]
        d = delta_rows[rows, :]
        a = jnp.zeros((block, HD), F32)
        for j in range(keys // step):
            cols = slice(j * step, (j + 1) * step)
            dp = dot(u, value_ref[cols, :], 1, 1)
            w = weights[rows, cols]
            g = [
                (w[:, n * HD : (n + 1) * HD] * (dp[:, n * HD : (n + 1) * HD] - d)).astype(BF16)
                for n in range(step // HD)
            ]
            a = a + dot(jnp.concatenate(g, axis=1), key_ref[cols, :], 1, 0)
        local[2, rows, :] = a
        return carry

    lax.fori_loop(0, heads * tokens // block, backward, 0)

    take_line(stat_out, stat_in, stat_send, stat_recv)
    top = stat_in[0, :heads]
    for n in range(1, pre_count):
        top = jnp.maximum(top, stat_in[n, :heads])
    mass = jnp.zeros((heads, tokens), F32)
    mean = jnp.zeros((heads, tokens), F32)
    for n in range(pre_count):
        share = jnp.exp2(stat_in[n, :heads] - top)
        mass = mass + share
        mean = mean + share * stat_in[n, heads:]
    stat[:heads, :] = top + jnp.log(mass) * LOG2E
    stat[heads : 2 * heads, :] = mean / mass
    table = stat[...].T
    for h in range(heads):
        rows = slice(h * tokens, (h + 1) * tokens)
        factor = jnp.exp2(high_rows[rows, :] - table[:, h : h + 1])
        shift = delta_rows[rows, :] - table[:, heads + h : heads + h + 1]
        part[0, rows, :] = (local[2, rows, :] + shift * local[1, rows, :]) * (factor * score_scale)
        part[1, rows, :] = local[0, rows, :] * factor

    def own_part(which, flow, distance):
        chunk = (pre + (distance if flow == 0 else pre_count - distance)) % pre_count
        return part[which, pl.ds(pl.multiple_of(chunk * own_rows, own_rows), own_rows), :]

    def hop(flow, distance):
        return (pre + (distance if flow == 0 else pre_count - distance)) % pre_count

    def chain_copy(flow, t, which):
        return remote(
            chain_out.at[flow, t, which],
            chain_in.at[flow, t, which],
            chain_send.at[flow, t, which],
            chain_recv.at[flow, t, which],
            hop(flow, 2),
            row,
        )

    def odd_copy(flow, t, which):
        return remote(
            odd_out.at[flow, t, which],
            odd_in.at[flow, t, which],
            odd_send.at[flow, t, which],
            odd_recv.at[flow, t, which],
            hop(flow, 1),
            row,
        )

    sent = []
    for t in range(steps):
        for which in (0, 1):
            if t == 0:
                chain_out[1, 0, which] = own_part(which, 1, half).astype(BF16)
                sent.append(chain_copy(1, 0, which))
                sent[-1].start()
            for flow in (0, 1):
                odd_out[flow, t, which] = own_part(which, flow, half - 1 - 2 * t).astype(BF16)
                sent.append(odd_copy(flow, t, which))
                sent[-1].start()
    for t in range(1, steps):
        for which in (0, 1):
            for flow in (0, 1):
                total = own_part(which, flow, half - 2 * t)
                odd_copy(flow, t - 1, which).wait_recv()
                total = total + odd_in[flow, t - 1, which].astype(F32)
                if flow == 1 or t > 1:
                    chain_copy(flow, t - 1, which).wait_recv()
                    total = total + chain_in[flow, t - 1, which].astype(F32)
                chain_out[flow, t, which] = total.astype(BF16)
                sent.append(chain_copy(flow, t, which))
                sent[-1].start()

    head = pre // pieces
    piece = pre % pieces
    results = []
    for which in (0, 1):
        total = own_part(which, 0, 0)
        for flow in (0, 1):
            odd_copy(flow, steps - 1, which).wait_recv()
            total = total + odd_in[flow, steps - 1, which].astype(F32)
            if flow == 1 or steps > 1:
                chain_copy(flow, steps - 1, which).wait_recv()
                total = total + chain_in[flow, steps - 1, which].astype(F32)
        results.append(total.astype(BF16))
        if which == 0:
            grad_q = jnp.concatenate([results[0]] * pieces, axis=0)
            piece_of = lax.broadcasted_iota(jnp.int32, (tokens, HD), 0) // own_rows
            grad_q = jnp.where(piece_of == piece, grad_q.astype(F32), 0.0).astype(BF16)
            up_head = up_ref[:, pl.ds(pl.multiple_of(head * HD, HD), HD)]
            term_out[:RANK, :] = (ADAPTER_SCALE * dot(up_head, grad_q, 1, 1)).astype(BF16)
            term_out[RANK:, :] = (ADAPTER_SCALE * dot(latent_ref[...], grad_q, 1, 0)).astype(BF16)
            term_copies = line_copies(term_out, term_in, term_send, term_recv)
            for copy in term_copies:
                copy.start()
            term_in[pre] = term_out[...]
    att_in[pre] = results[1]

    stride = max(pre_count // 4, 1)
    far = [k for k in (2 * stride, stride, 3 * stride) if k < pre_count]
    near = [k if k <= stride // 2 else k - stride for k in range(1, stride)]

    def att_copy(slot, n, k):
        return remote(
            att_in.at[slot],
            att_in.at[slot],
            att_send.at[n],
            att_recv.at[slot],
            (pre + k + pre_count) % pre_count,
            row,
        )

    att_copies = [att_copy(pre, n, k) for n, k in enumerate(far)]
    for copy in att_copies:
        copy.start()

    load.wait()
    take_line(term_out, term_in, term_send, term_recv)
    code = jnp.zeros((RANK, tokens), F32)
    for h in range(heads):
        lifted = jnp.zeros((RANK, HD), F32)
        for n in range(pieces):
            code = code + term_in[h * pieces + n, :RANK, :].astype(F32)
            lifted = lifted + term_in[h * pieces + n, RANK:, :].astype(F32)
        raised[:, h * HD : (h + 1) * HD] = lifted
    for n in range(per_student):
        quarter_out[n] = raised[:, n * width : (n + 1) * width].astype(BF16)

    def quarter_copy(k):
        to = (place + k) % per_student
        return remote(
            quarter_out.at[to],
            quarter_in.at[place],
            quarter_send.at[k],
            quarter_recv.at[place],
            pre,
            first_row + to,
        )

    for k in range(1, per_student):
        quarter_copy(k).start()
    quarter_in[place] = quarter_out[place]
    code = code.astype(BF16)

    grad_copies = []
    for n, offset in enumerate(plane):
        to = plane_peer(row, extent, offset)
        cols = pl.ds(pl.multiple_of(to * depth, depth), depth)
        grad_out[to] = dot(code, hidden[:, cols], 1, 0).astype(BF16)
        grad_copies.append(
            remote(grad_out.at[to], grad_in.at[row], grad_send.at[n], grad_recv.at[row], pre, to)
        )
        grad_copies[-1].start()
    cols = pl.ds(pl.multiple_of(row * depth, depth), depth)
    grad_in[row] = dot(code, hidden[:, cols], 1, 0).astype(BF16)

    for k in range(1, per_student):
        origin = (place + k) % per_student
        remote(
            quarter_out.at[0],
            quarter_in.at[origin],
            quarter_send.at[0],
            quarter_recv.at[origin],
            pre,
            row,
        ).wait_recv()
    summed = jnp.zeros((RANK, width), F32)
    for n in range(per_student):
        summed = summed + quarter_in[n].astype(F32)
    up_out[...] = summed.astype(BF16)
    up_copies = []
    for n, offset in enumerate(plane):
        to = plane_peer(row, extent, offset)
        up_copies.append(
            remote(up_out, up_in.at[row], up_send.at[n], up_recv.at[row], pre, to)
        )
        up_copies[-1].start()
    up_in[row] = up_out[...]

    def slot_wait(landing, slot, send_sem, recv_sem):
        remote(
            landing.at[slot], landing.at[slot], send_sem.at[0], recv_sem.at[slot], pre, row
        ).wait_recv()

    for k in far:
        slot_wait(att_in, (pre + k) % pre_count, att_send, att_recv)
    for k in near:
        for n in range(len(far) + 1):
            slot = (pre + n * stride) % pre_count
            att_copies.append(att_copy(slot, len(att_copies), k))
            att_copies[-1].start()

    def take_grad(k, carry):
        slot_wait(grad_in, (row + k) % row_count, grad_send, grad_recv)
        return carry

    lax.fori_loop(1, row_count, take_grad, 0)
    grad_ref[...] = grad_in[...]
    for k in near:
        for n in range(len(far) + 1):
            slot = (pre - k + n * stride + pre_count) % pre_count
            slot_wait(att_in, slot, att_send, att_recv)
    attended_ref[...] = att_in[...]

    def take_up(k, carry):
        slot_wait(up_in, (row + k) % row_count, up_send, up_recv)
        return carry

    lax.fori_loop(1, row_count, take_up, 0)
    raised_ref[...] = up_in[...]

    for copy in stat_copies + sent + term_copies + att_copies + grad_copies + up_copies:
        copy.wait_send()
    for k in range(1, per_student):
        quarter_copy(k).wait_send()


def output_kernel(
    per_student, ids_ref, att_ref, grad_ref, raised_ref, attended_ref, grad_a_ref, grad_up_ref, rows, ups
):
    count, own_rows, _ = att_ref.shape
    tokens = attended_ref.shape[0]
    pieces = tokens // own_rows
    students = grad_ref.shape[0] // per_student
    width = raised_ref.shape[2]
    pick = picker(ids_ref, students, students * RANK)
    for s in range(students):
        block_sum = grad_ref[s * per_student].astype(F32)
        for n in range(1, per_student):
            block_sum = block_sum + grad_ref[s * per_student + n].astype(F32)
        for n, piece in enumerate(split_parts(block_sum, 2)):
            rows[n, s * RANK : (s + 1) * RANK, :] = piece.astype(BF16)
        for j in range(per_student):
            ups[s * RANK : (s + 1) * RANK, j * width : (j + 1) * width] = raised_ref[
                s * per_student + j
            ]
    grad_a_ref[...] = dot(rows[0], pick, 0, 0) + dot(rows[1], pick, 0, 0)
    grad_up_ref[...] = dot(pick, ups[...], 0, 0)
    for c in range(count):
        h, n = c // pieces, c % pieces
        attended_ref[n * own_rows : (n + 1) * own_rows, h * HD : (h + 1) * HD] = att_ref[c]


def vmem():
    return pl.BlockSpec(memory_space=pltpu.VMEM)


def smem():
    return pl.BlockSpec(memory_space=pltpu.SMEM)


def anywhere():
    return pl.BlockSpec(memory_space=pl.ANY)


def shards(
    pre_count,
    row_count,
    hidden_in,
    frozen_query_base,
    k_prefix,
    v_prefix,
    tree_mask,
    adapter_ids,
    a_down,
    up_weight_matrix,
    cotangent,
):
    tokens, width = frozen_query_base.shape
    model = hidden_in.shape[1]
    heads = width // HD
    keys = k_prefix.shape[0]
    depth, ranks = a_down.shape
    students = tree_mask.shape[0]
    per_student = row_count // students
    dma = pltpu.SemaphoreType.DMA
    latent, queries, own_up = pl.pallas_call(
        functools.partial(query_kernel, per_student, row_count),
        out_shape=(
            jax.ShapeDtypeStruct((RANK, tokens), BF16),
            jax.ShapeDtypeStruct((tokens, width), BF16),
            jax.ShapeDtypeStruct((RANK, width), BF16),
        ),
        in_specs=[smem(), vmem(), anywhere(), vmem(), vmem()],
        out_specs=(vmem(), vmem(), vmem()),
        scratch_shapes=[
            pltpu.VMEM((students, RANK, depth), BF16),
            pltpu.VMEM((row_count, RANK, depth), BF16),
            pltpu.VMEM((tokens, model), BF16),
            dma((row_count,)),
            dma((row_count,)),
            dma,
        ],
        compiler_params=pltpu.CompilerParams(collective_id=0, has_side_effects=True),
        name="queries",
    )(adapter_ids, a_down, hidden_in, up_weight_matrix, frozen_query_base)

    rows = heads * tokens
    own_rows = rows // pre_count
    steps = pre_count // 4
    quarter = width // per_student
    ring = (2, steps, 2)
    att, grad, raised = pl.pallas_call(
        functools.partial(attention_kernel, pre_count, row_count, per_student),
        out_shape=(
            jax.ShapeDtypeStruct((pre_count, own_rows, HD), BF16),
            jax.ShapeDtypeStruct((row_count, RANK, depth), BF16),
            jax.ShapeDtypeStruct((row_count, RANK, quarter), BF16),
        ),
        in_specs=[smem()] + [vmem()] * 6 + [anywhere()],
        out_specs=(vmem(), vmem(), vmem()),
        scratch_shapes=[
            pltpu.VMEM((tokens, model), BF16),
            pltpu.VMEM((rows, HD), BF16),
            pltpu.VMEM((rows, HD), BF16),
            pltpu.VMEM((8, keys), F32),
            pltpu.VMEM((keys, 2 * HD), BF16),
            pltpu.VMEM((rows, keys), F32),
            pltpu.VMEM((rows, HD), F32),
            pltpu.VMEM((rows, HD), F32),
            pltpu.VMEM((3, rows, HD), F32),
            pltpu.VMEM((2, rows, HD), F32),
            pltpu.VMEM((tokens, HD), F32),
            pltpu.VMEM((2 * heads, tokens), F32),
            pltpu.VMEM((pre_count, 2 * heads, tokens), F32),
            pltpu.VMEM(ring + (own_rows, HD), BF16),
            pltpu.VMEM(ring + (own_rows, HD), BF16),
            pltpu.VMEM(ring + (own_rows, HD), BF16),
            pltpu.VMEM(ring + (own_rows, HD), BF16),
            pltpu.VMEM((2 * RANK, HD), BF16),
            pltpu.VMEM((pre_count, 2 * RANK, HD), BF16),
            pltpu.VMEM((pre_count, own_rows, HD), BF16),
            pltpu.VMEM((per_student, RANK, quarter), BF16),
            pltpu.VMEM((per_student, RANK, quarter), BF16),
            pltpu.VMEM((row_count, RANK, depth), BF16),
            pltpu.VMEM((row_count, RANK, depth), BF16),
            pltpu.VMEM((RANK, quarter), BF16),
            pltpu.VMEM((row_count, RANK, quarter), BF16),
            pltpu.VMEM((RANK, width), F32),
            dma,
            dma((pre_count,)),
            dma((pre_count,)),
            dma(ring),
            dma(ring),
            dma(ring),
            dma(ring),
            dma((pre_count,)),
            dma((pre_count,)),
            dma((pre_count,)),
            dma((pre_count,)),
            dma((per_student,)),
            dma((per_student,)),
            dma((row_count,)),
            dma((row_count,)),
            dma((row_count,)),
            dma((row_count,)),
        ],
        compiler_params=pltpu.CompilerParams(collective_id=1, has_side_effects=True),
        name="attention",
    )(tree_mask, queries, cotangent, k_prefix, v_prefix, latent, own_up, hidden_in)
    return pl.pallas_call(
        functools.partial(output_kernel, per_student),
        out_shape=(
            jax.ShapeDtypeStruct((tokens, width), BF16),
            jax.ShapeDtypeStruct((depth, ranks), F32),
            jax.ShapeDtypeStruct((ranks, width), F32),
        ),
        in_specs=[smem()] + [vmem()] * 3,
        out_specs=(vmem(), vmem(), vmem()),
        scratch_shapes=[
            pltpu.VMEM((2, ranks, depth), BF16),
            pltpu.VMEM((ranks, width), BF16),
        ],
        name="outputs",
    )(adapter_ids, att, grad, raised)


def solution(mesh):
    in_specs = (
        P("row", None),
        P("row", None),
        P("pre", None),
        P("pre", None),
        P(None, "pre"),
        P(),
        P("row", None),
        P(),
        P("row", None),
    )
    out_specs = (P("row", None), P("row", None), P())
    body = functools.partial(shards, mesh.shape["pre"], mesh.shape["row"])
    return jax.shard_map(body, mesh=mesh, in_specs=in_specs, out_specs=out_specs, check_vma=False)
```

```python
import functools
import math

import jax
import jax.numpy as jnp
from jax import lax
from jax.experimental import pallas as pl
from jax.experimental.pallas import tpu as pltpu
from jax.sharding import PartitionSpec as P

HD = 128
RANK = 16
MB = 128
ADAPTER_SCALE = 2.0
DEAD = -1e30
FLOOR = -1e29
TINY = 1e-30
STEP = 512
LOG2E = math.log2(math.e)
MESH = pl.DeviceIdType.MESH
F32 = jnp.float32
BF16 = jnp.bfloat16


def dot(a, b, ca, cb):
    return lax.dot_general(a, b, (((ca,), (cb,)), ((), ())), preferred_element_type=F32)


def remote(src, dst, send_sem, recv_sem, pre, row):
    return pltpu.make_async_remote_copy(
        src_ref=src,
        dst_ref=dst,
        send_sem=send_sem,
        recv_sem=recv_sem,
        device_id=(pre, row),
        device_id_type=MESH,
    )


def plane_offsets(row_count):
    extent = (4, 4, 2) if row_count == 32 else (1, row_count // 2, 2)
    around = lambda n, size: min(n, size - n)
    offsets = [
        (around(x, extent[0]) + around(y, extent[1]), x, y, c)
        for x in range(extent[0])
        for y in range(extent[1])
        for c in range(extent[2])
    ]
    return extent, [o[1:] for o in sorted(offsets, key=lambda o: -o[0]) if o[1:] != (0, 0, 0)]


def plane_peer(row, extent, offset):
    _, ys, cs = extent
    x = (row // (ys * cs) + offset[0]) % extent[0]
    y = (row // cs % ys + offset[1]) % ys
    return (x * ys + y) * cs + (row % cs + offset[2]) % cs


def line_offsets(count):
    return sorted(range(1, count), key=lambda k: -min(k, count - k))


def picker(ids_ref, students, ranks):
    place = lax.broadcasted_iota(jnp.int32, (ranks, ranks), 0)
    column = lax.broadcasted_iota(jnp.int32, (ranks, ranks), 1)
    wanted = jnp.zeros((ranks, ranks), jnp.int32)
    for s in range(students):
        wanted = jnp.where(place // RANK == s, ids_ref[s] * RANK + place % RANK, wanted)
    return jnp.where(column == wanted, 1.0, 0.0).astype(BF16)


def query_kernel(
    per_student,
    row_count,
    ids_ref,
    a_hbm,
    hidden_hbm,
    up_hbm,
    base_hbm,
    latent_ref,
    query_ref,
    own_up_ref,
    outgoing,
    incoming,
    a_rows,
    hidden,
    up_rows,
    base_rows,
    send_sem,
    recv_sem,
    load_sem,
):
    pre = lax.axis_index("pre")
    row = lax.axis_index("row")
    students = row_count // per_student
    depth, ranks = a_hbm.shape
    barrier = pltpu.get_barrier_semaphore()

    def greet(k, carry):
        pl.semaphore_signal(
            barrier, inc=1, device_id=(pre, (row + k) % row_count), device_id_type=MESH
        )
        return carry

    lax.fori_loop(1, row_count, greet, 0)
    loads = [
        pltpu.make_async_copy(source, landing, load_sem.at[n])
        for n, (source, landing) in enumerate(
            ((a_hbm, a_rows), (hidden_hbm, hidden), (up_hbm, up_rows), (base_hbm, base_rows))
        )
    ]
    for copy in loads:
        copy.start()
    pick = picker(ids_ref, students, ranks)
    loads[0].wait()
    picked = dot(pick, a_rows[...], 1, 1).astype(BF16)
    for s in range(students):
        outgoing[s] = picked[s * RANK : (s + 1) * RANK]
    pl.semaphore_wait(barrier, row_count - 1)

    extent, offsets = plane_offsets(row_count)
    own_cols = pl.ds(pl.multiple_of(row * depth, depth), depth)
    copies = []
    for k, offset in enumerate(offsets):
        to = plane_peer(row, extent, offset)
        copies.append(
            remote(
                outgoing.at[to // per_student],
                incoming.at[:, own_cols],
                send_sem.at[k],
                recv_sem.at[row],
                pre,
                to,
            )
        )
        copies[-1].start()
    mine = row // per_student
    incoming[:, own_cols] = outgoing[mine]
    place = lax.broadcasted_iota(jnp.int32, (RANK, ranks), 0)
    column = lax.broadcasted_iota(jnp.int32, (RANK, ranks), 1)
    own_pick = jnp.where(column == ids_ref[mine] * RANK + place, 1.0, 0.0).astype(BF16)
    for copy in loads[1:]:
        copy.wait()
    up = dot(own_pick, up_rows[...], 1, 0).astype(BF16)
    own_up_ref[...] = up

    def take(k, carry):
        source = (row + k) % row_count
        cols = pl.ds(pl.multiple_of(source * depth, depth), depth)
        remote(
            outgoing.at[0], incoming.at[:, cols], send_sem.at[0], recv_sem.at[source], pre, row
        ).wait_recv()
        return carry

    lax.fori_loop(1, row_count, take, 0)
    total = dot(incoming[...], hidden[...], 1, 1)
    latent = total.astype(BF16)
    latent_ref[...] = latent
    raised = dot(latent, up, 0, 0)
    query_ref[...] = (base_rows[...].astype(F32) + ADAPTER_SCALE * raised).astype(BF16)

    for copy in copies:
        copy.wait_send()


def split_parts(x, count):
    parts = []
    for _ in range(count):
        part = x.astype(BF16).astype(F32)
        parts.append(part)
        x = x - part
    return parts


def attention_kernel(
    pre_count,
    row_count,
    per_student,
    mask_ref,
    query_hbm,
    upstream_hbm,
    key_hbm,
    value_hbm,
    latent_ref,
    up_ref,
    hidden_hbm,
    attended_ref,
    grad_ref,
    raised_ref,
    hidden,
    q_rows,
    u_rows,
    bias,
    value_key,
    weights,
    high_rows,
    delta_rows,
    sum_rows,
    both_rows,
    back_rows,
    part,
    stat,
    stat_out,
    stat_in,
    chain_out,
    chain_in,
    odd_out,
    odd_in,
    term_out,
    term_in,
    att_in,
    quarter_out,
    quarter_in,
    grad_out,
    grad_in,
    up_out,
    up_in,
    raised,
    load_sem,
    input_sem,
    stat_send,
    stat_recv,
    chain_send,
    chain_recv,
    odd_send,
    odd_recv,
    term_send,
    term_recv,
    att_send,
    att_recv,
    quarter_send,
    quarter_recv,
    grad_send,
    grad_recv,
    up_send,
    up_recv,
):
    pre = lax.axis_index("pre")
    row = lax.axis_index("row")
    tokens = query_hbm.shape[0]
    heads = query_hbm.shape[1] // HD
    keys = key_hbm.shape[0]
    own_rows = heads * tokens // pre_count
    pieces = tokens // own_rows
    half = pre_count // 2
    steps = half // 2
    score_scale = 1.0 / math.sqrt(HD)
    fold = score_scale * LOG2E
    student = row // per_student
    place = row % per_student
    first_row = student * per_student
    depth = grad_out.shape[2]
    width = heads * HD // per_student
    extent, plane = plane_offsets(row_count)
    line = line_offsets(pre_count)
    barrier = pltpu.get_barrier_semaphore()

    loads = [
        pltpu.make_async_copy(key_hbm, value_key.at[:, HD:], input_sem.at[0]),
        pltpu.make_async_copy(value_hbm, value_key.at[:, :HD], input_sem.at[1]),
    ]
    for n, (source, landing) in enumerate(((query_hbm, q_rows), (upstream_hbm, u_rows))):
        for h in range(heads):
            loads.append(
                pltpu.make_async_copy(
                    source.at[:, h * HD : (h + 1) * HD],
                    landing.at[h * tokens : (h + 1) * tokens, :],
                    input_sem.at[2 + n * heads + h],
                )
            )
    for copy in loads:
        copy.start()
    load = pltpu.make_async_copy(hidden_hbm, hidden, load_sem)
    load.start()
    for k in line:
        pl.semaphore_signal(
            barrier, inc=1, device_id=((pre + k) % pre_count, row), device_id_type=MESH
        )
    for offset in plane:
        pl.semaphore_signal(
            barrier, inc=1, device_id=(pre, plane_peer(row, extent, offset)), device_id_type=MESH
        )

    for b in range(keys // MB):
        read = jnp.full((8, MB), mask_ref[student, b], jnp.int32)
        bias[:, b * MB : (b + 1) * MB] = jnp.where(read > 0, 0.0, DEAD)
    rows_all = heads * tokens
    step = weights.shape[2]
    lane = lax.broadcasted_iota(jnp.int32, (tokens, HD), 1)
    high_rows[...] = jnp.full((rows_all, HD), FLOOR, F32)
    for copy in loads:
        copy.wait()

    def score(j, carry):
        cols = pl.ds(pl.multiple_of(j * step, step), step)
        s = dot(q_rows[...], value_key[cols, HD:], 1, 1) + bias[0:1, cols]
        weights[j] = s
        high = high_rows[...]
        for g in range(step // HD):
            high = jnp.maximum(high, s[:, g * HD : (g + 1) * HD])
        high_rows[...] = high
        return carry

    lax.fori_loop(0, keys // step, score, 0)
    top = jnp.max(high_rows[...], axis=1, keepdims=True) * fold
    high_rows[...] = jnp.broadcast_to(top, (rows_all, HD))
    sum_rows[...] = jnp.zeros((rows_all, HD), F32)
    both_rows[...] = jnp.zeros((rows_all, 2 * HD), F32)

    def weigh(j, carry):
        cols = pl.ds(pl.multiple_of(j * step, step), step)
        level = high_rows[...]
        sums = sum_rows[...]
        ws = []
        for g in range(step // HD):
            w = jnp.exp2(weights[j, :, g * HD : (g + 1) * HD] * fold - level)
            weights[j, :, g * HD : (g + 1) * HD] = w
            sums = sums + w
            ws.append(w.astype(BF16))
        sum_rows[...] = sums
        both_rows[...] += dot(jnp.concatenate(ws, axis=1), value_key[cols, :], 1, 0)
        return carry

    lax.fori_loop(0, keys // step, weigh, 0)
    table = jnp.zeros((tokens, HD), F32)
    for h in range(heads):
        rows = slice(h * tokens, (h + 1) * tokens)
        l = jnp.maximum(jnp.sum(sum_rows[rows, :], axis=1, keepdims=True), TINY)
        weighed = u_rows[rows, :].astype(F32) * both_rows[rows, :HD]
        d = jnp.sum(weighed, axis=1, keepdims=True) / l
        lse = high_rows[rows, :] + jnp.log(l) * LOG2E
        delta_rows[rows, :] = jnp.broadcast_to(d, (tokens, HD))
        table = jnp.where(lane == h, lse, table)
        table = jnp.where(lane == heads + h, d, table)
    stat[...] = table

    stat_out[...] = stat[...].T[: 2 * heads]
    stat_in[pre] = stat_out[...]
    pl.semaphore_wait(barrier, row_count - 1 + pre_count - 1)

    def line_copies(source, landing, send_sem, recv_sem):
        return [
            remote(
                source,
                landing.at[pre],
                send_sem.at[n],
                recv_sem.at[pre],
                (pre + k) % pre_count,
                row,
            )
            for n, k in enumerate(line)
        ]

    def take_line(source, landing, send_sem, recv_sem):
        for k in reversed(line):
            origin = (pre + k) % pre_count
            remote(
                source, landing.at[origin], send_sem.at[0], recv_sem.at[origin], pre, row
            ).wait_recv()

    stat_copies = line_copies(stat_out, stat_in, stat_send, stat_recv)
    for copy in stat_copies:
        copy.start()

    back_rows[...] = jnp.zeros((rows_all, HD), F32)

    def backward(j, carry):
        cols = pl.ds(pl.multiple_of(j * step, step), step)
        dp = dot(u_rows[...], value_key[cols, :HD], 1, 1)
        d = delta_rows[...]
        g = [
            (weights[j, :, n * HD : (n + 1) * HD] * (dp[:, n * HD : (n + 1) * HD] - d)).astype(BF16)
            for n in range(step // HD)
        ]
        back_rows[...] += dot(jnp.concatenate(g, axis=1), value_key[cols, HD:], 1, 0)
        return carry

    lax.fori_loop(0, keys // step, backward, 0)

    take_line(stat_out, stat_in, stat_send, stat_recv)
    top = stat_in[0, :heads]
    for n in range(1, pre_count):
        top = jnp.maximum(top, stat_in[n, :heads])
    mass = jnp.zeros((heads, tokens), F32)
    mean = jnp.zeros((heads, tokens), F32)
    for n in range(pre_count):
        share = jnp.exp2(stat_in[n, :heads] - top)
        mass = mass + share
        mean = mean + share * stat_in[n, heads:]
    stat[:heads, :] = top + jnp.log(mass) * LOG2E
    stat[heads : 2 * heads, :] = mean / mass
    table = stat[...].T
    for h in range(heads):
        rows = slice(h * tokens, (h + 1) * tokens)
        factor = jnp.exp2(high_rows[rows, :] - table[:, h : h + 1])
        shift = delta_rows[rows, :] - table[:, heads + h : heads + h + 1]
        part[0, rows, :] = (back_rows[rows, :] + shift * both_rows[rows, HD:]) * (factor * score_scale)
        part[1, rows, :] = both_rows[rows, :HD] * factor

    def own_part(which, flow, distance):
        chunk = (pre + (distance if flow == 0 else pre_count - distance)) % pre_count
        return part[which, pl.ds(pl.multiple_of(chunk * own_rows, own_rows), own_rows), :]

    def hop(flow, distance):
        return (pre + (distance if flow == 0 else pre_count - distance)) % pre_count

    def chain_copy(flow, t, which):
        return remote(
            chain_out.at[flow, t, which],
            chain_in.at[flow, t, which],
            chain_send.at[flow, t, which],
            chain_recv.at[flow, t, which],
            hop(flow, 2),
            row,
        )

    def odd_copy(flow, t, which):
        return remote(
            odd_out.at[flow, t, which],
            odd_in.at[flow, t, which],
            odd_send.at[flow, t, which],
            odd_recv.at[flow, t, which],
            hop(flow, 1),
            row,
        )

    sent = []

    def start_sums(which):
        chain_out[1, 0, which] = own_part(which, 1, half).astype(BF16)
        sent.append(chain_copy(1, 0, which))
        sent[-1].start()
        for t in range(steps):
            for flow in (0, 1):
                odd_out[flow, t, which] = own_part(which, flow, half - 1 - 2 * t).astype(BF16)
                sent.append(odd_copy(flow, t, which))
                sent[-1].start()

    def arrivals(flow, t, which, total):
        odd_copy(flow, t, which).wait_recv()
        total = total + odd_in[flow, t, which].astype(F32)
        if flow == 1 or t > 0:
            chain_copy(flow, t, which).wait_recv()
            total = total + chain_in[flow, t, which].astype(F32)
        return total

    def relay(t, which):
        for flow in (1, 0):
            total = arrivals(flow, t - 1, which, own_part(which, flow, half - 2 * t))
            chain_out[flow, t, which] = total.astype(BF16)
            sent.append(chain_copy(flow, t, which))
            sent[-1].start()

    def own_sum(which):
        total = own_part(which, 0, 0)
        for flow in (0, 1):
            total = arrivals(flow, steps - 1, which, total)
        return total.astype(BF16)

    start_sums(0)
    for t in range(1, steps):
        relay(t, 0)
        if t == 1:
            start_sums(1)
        else:
            relay(t - 1, 1)
    if steps == 1:
        start_sums(1)

    head = pre // pieces
    piece = pre % pieces
    own = own_sum(0)
    grad_q = jnp.concatenate([own] * pieces, axis=0)
    piece_of = lax.broadcasted_iota(jnp.int32, (tokens, HD), 0) // own_rows
    grad_q = jnp.where(piece_of == piece, grad_q.astype(F32), 0.0).astype(BF16)
    up_head = up_ref[:, pl.ds(pl.multiple_of(head * HD, HD), HD)]
    term_out[:RANK, :] = (ADAPTER_SCALE * dot(up_head, grad_q, 1, 1)).astype(BF16)
    term_out[RANK:, :] = (ADAPTER_SCALE * dot(latent_ref[...], grad_q, 1, 0)).astype(BF16)
    term_copies = line_copies(term_out, term_in, term_send, term_recv)
    for copy in term_copies:
        copy.start()
    term_in[pre] = term_out[...]
    if steps > 1:
        relay(steps - 1, 1)
    att_in[pre] = own_sum(1)

    stride = max(pre_count // 4, 1)
    far = [k for k in (2 * stride, stride, 3 * stride) if k < pre_count]
    near = [k if k <= stride // 2 else k - stride for k in range(1, stride)]

    def att_copy(slot, n, k):
        return remote(
            att_in.at[slot],
            att_in.at[slot],
            att_send.at[n],
            att_recv.at[slot],
            (pre + k + pre_count) % pre_count,
            row,
        )

    att_copies = [att_copy(pre, n, k) for n, k in enumerate(far)]
    for copy in att_copies:
        copy.start()

    load.wait()
    take_line(term_out, term_in, term_send, term_recv)
    code = jnp.zeros((RANK, tokens), F32)
    for h in range(heads):
        lifted = jnp.zeros((RANK, HD), F32)
        for n in range(pieces):
            code = code + term_in[h * pieces + n, :RANK, :].astype(F32)
            lifted = lifted + term_in[h * pieces + n, RANK:, :].astype(F32)
        raised[:, h * HD : (h + 1) * HD] = lifted
    for n in range(per_student):
        quarter_out[n] = raised[:, n * width : (n + 1) * width].astype(BF16)

    def quarter_copy(k):
        to = (place + k) % per_student
        return remote(
            quarter_out.at[to],
            quarter_in.at[place],
            quarter_send.at[k],
            quarter_recv.at[place],
            pre,
            first_row + to,
        )

    for k in range(1, per_student):
        quarter_copy(k).start()
    quarter_in[place] = quarter_out[place]
    code = code.astype(BF16)

    grad_copies = []
    for n, offset in enumerate(plane):
        to = plane_peer(row, extent, offset)
        cols = pl.ds(pl.multiple_of(to * depth, depth), depth)
        grad_out[to] = dot(code, hidden[:, cols], 1, 0).astype(BF16)
        grad_copies.append(
            remote(grad_out.at[to], grad_in.at[row], grad_send.at[n], grad_recv.at[row], pre, to)
        )
        grad_copies[-1].start()
    cols = pl.ds(pl.multiple_of(row * depth, depth), depth)
    grad_in[row] = dot(code, hidden[:, cols], 1, 0).astype(BF16)

    for k in range(1, per_student):
        origin = (place + k) % per_student
        remote(
            quarter_out.at[0],
            quarter_in.at[origin],
            quarter_send.at[0],
            quarter_recv.at[origin],
            pre,
            row,
        ).wait_recv()
    summed = jnp.zeros((RANK, width), F32)
    for n in range(per_student):
        summed = summed + quarter_in[n].astype(F32)
    up_out[...] = summed.astype(BF16)
    up_copies = []
    for n, offset in enumerate(plane):
        to = plane_peer(row, extent, offset)
        up_copies.append(
            remote(up_out, up_in.at[row], up_send.at[n], up_recv.at[row], pre, to)
        )
        up_copies[-1].start()
    up_in[row] = up_out[...]

    def slot_wait(landing, slot, send_sem, recv_sem):
        remote(
            landing.at[slot], landing.at[slot], send_sem.at[0], recv_sem.at[slot], pre, row
        ).wait_recv()

    for k in far:
        slot_wait(att_in, (pre + k) % pre_count, att_send, att_recv)
    for k in near:
        for n in range(len(far) + 1):
            slot = (pre + n * stride) % pre_count
            att_copies.append(att_copy(slot, len(att_copies), k))
            att_copies[-1].start()

    def take_grad(k, carry):
        slot_wait(grad_in, (row + k) % row_count, grad_send, grad_recv)
        return carry

    lax.fori_loop(1, row_count, take_grad, 0)
    grad_ref[...] = grad_in[...]
    for k in near:
        for n in range(len(far) + 1):
            slot = (pre - k + n * stride + pre_count) % pre_count
            slot_wait(att_in, slot, att_send, att_recv)
    attended_ref[...] = att_in[...]

    def take_up(k, carry):
        slot_wait(up_in, (row + k) % row_count, up_send, up_recv)
        return carry

    lax.fori_loop(1, row_count, take_up, 0)
    raised_ref[...] = up_in[...]

    for copy in stat_copies + sent + term_copies + att_copies + grad_copies + up_copies:
        copy.wait_send()
    for k in range(1, per_student):
        quarter_copy(k).wait_send()


def output_kernel(
    per_student, ids_ref, att_ref, grad_ref, raised_ref, attended_ref, grad_a_ref, grad_up_ref, rows, ups
):
    count, own_rows, _ = att_ref.shape
    tokens = attended_ref.shape[0]
    pieces = tokens // own_rows
    students = grad_ref.shape[0] // per_student
    width = raised_ref.shape[2]
    pick = picker(ids_ref, students, students * RANK)
    for s in range(students):
        block_sum = grad_ref[s * per_student].astype(F32)
        for n in range(1, per_student):
            block_sum = block_sum + grad_ref[s * per_student + n].astype(F32)
        for n, piece in enumerate(split_parts(block_sum, 2)):
            rows[n, s * RANK : (s + 1) * RANK, :] = piece.astype(BF16)
        for j in range(per_student):
            ups[s * RANK : (s + 1) * RANK, j * width : (j + 1) * width] = raised_ref[
                s * per_student + j
            ]
    grad_a_ref[...] = dot(rows[0], pick, 0, 0) + dot(rows[1], pick, 0, 0)
    grad_up_ref[...] = dot(pick, ups[...], 0, 0)
    for c in range(count):
        h, n = c // pieces, c % pieces
        attended_ref[n * own_rows : (n + 1) * own_rows, h * HD : (h + 1) * HD] = att_ref[c]


def vmem():
    return pl.BlockSpec(memory_space=pltpu.VMEM)


def smem():
    return pl.BlockSpec(memory_space=pltpu.SMEM)


def anywhere():
    return pl.BlockSpec(memory_space=pl.ANY)


def shards(
    pre_count,
    row_count,
    hidden_in,
    frozen_query_base,
    k_prefix,
    v_prefix,
    tree_mask,
    adapter_ids,
    a_down,
    up_weight_matrix,
    cotangent,
):
    tokens, width = frozen_query_base.shape
    model = hidden_in.shape[1]
    heads = width // HD
    keys = k_prefix.shape[0]
    depth, ranks = a_down.shape
    students = tree_mask.shape[0]
    per_student = row_count // students
    dma = pltpu.SemaphoreType.DMA
    latent, queries, own_up = pl.pallas_call(
        functools.partial(query_kernel, per_student, row_count),
        out_shape=(
            jax.ShapeDtypeStruct((RANK, tokens), BF16),
            jax.ShapeDtypeStruct((tokens, width), BF16),
            jax.ShapeDtypeStruct((RANK, width), BF16),
        ),
        in_specs=[smem()] + [anywhere()] * 4,
        out_specs=(vmem(), vmem(), vmem()),
        scratch_shapes=[
            pltpu.VMEM((students, RANK, depth), BF16),
            pltpu.VMEM((RANK, model), BF16),
            pltpu.VMEM((depth, ranks), BF16),
            pltpu.VMEM((tokens, model), BF16),
            pltpu.VMEM((ranks, width), BF16),
            pltpu.VMEM((tokens, width), BF16),
            dma((row_count,)),
            dma((row_count,)),
            dma((4,)),
        ],
        compiler_params=pltpu.CompilerParams(collective_id=0, has_side_effects=True),
        name="queries",
    )(adapter_ids, a_down, hidden_in, up_weight_matrix, frozen_query_base)

    rows = heads * tokens
    own_rows = rows // pre_count
    steps = pre_count // 4
    quarter = width // per_student
    ring = (2, steps, 2)
    att, grad, raised = pl.pallas_call(
        functools.partial(attention_kernel, pre_count, row_count, per_student),
        out_shape=(
            jax.ShapeDtypeStruct((pre_count, own_rows, HD), BF16),
            jax.ShapeDtypeStruct((row_count, RANK, depth), BF16),
            jax.ShapeDtypeStruct((row_count, RANK, quarter), BF16),
        ),
        in_specs=[smem()] + [anywhere()] * 4 + [vmem()] * 2 + [anywhere()],
        out_specs=(vmem(), vmem(), vmem()),
        scratch_shapes=[
            pltpu.VMEM((tokens, model), BF16),
            pltpu.VMEM((rows, HD), BF16),
            pltpu.VMEM((rows, HD), BF16),
            pltpu.VMEM((8, keys), F32),
            pltpu.VMEM((keys, 2 * HD), BF16),
            pltpu.VMEM((keys // STEP, rows, STEP), F32),
            pltpu.VMEM((rows, HD), F32),
            pltpu.VMEM((rows, HD), F32),
            pltpu.VMEM((rows, HD), F32),
            pltpu.VMEM((rows, 2 * HD), F32),
            pltpu.VMEM((rows, HD), F32),
            pltpu.VMEM((2, rows, HD), F32),
            pltpu.VMEM((tokens, HD), F32),
            pltpu.VMEM((2 * heads, tokens), F32),
            pltpu.VMEM((pre_count, 2 * heads, tokens), F32),
            pltpu.VMEM(ring + (own_rows, HD), BF16),
            pltpu.VMEM(ring + (own_rows, HD), BF16),
            pltpu.VMEM(ring + (own_rows, HD), BF16),
            pltpu.VMEM(ring + (own_rows, HD), BF16),
            pltpu.VMEM((2 * RANK, HD), BF16),
            pltpu.VMEM((pre_count, 2 * RANK, HD), BF16),
            pltpu.VMEM((pre_count, own_rows, HD), BF16),
            pltpu.VMEM((per_student, RANK, quarter), BF16),
            pltpu.VMEM((per_student, RANK, quarter), BF16),
            pltpu.VMEM((row_count, RANK, depth), BF16),
            pltpu.VMEM((row_count, RANK, depth), BF16),
            pltpu.VMEM((RANK, quarter), BF16),
            pltpu.VMEM((row_count, RANK, quarter), BF16),
            pltpu.VMEM((RANK, width), F32),
            dma,
            dma((2 + 2 * heads,)),
            dma((pre_count,)),
            dma((pre_count,)),
            dma(ring),
            dma(ring),
            dma(ring),
            dma(ring),
            dma((pre_count,)),
            dma((pre_count,)),
            dma((pre_count,)),
            dma((pre_count,)),
            dma((per_student,)),
            dma((per_student,)),
            dma((row_count,)),
            dma((row_count,)),
            dma((row_count,)),
            dma((row_count,)),
        ],
        compiler_params=pltpu.CompilerParams(collective_id=1, has_side_effects=True),
        name="attention",
    )(tree_mask, queries, cotangent, k_prefix, v_prefix, latent, own_up, hidden_in)
    return pl.pallas_call(
        functools.partial(output_kernel, per_student),
        out_shape=(
            jax.ShapeDtypeStruct((tokens, width), BF16),
            jax.ShapeDtypeStruct((depth, ranks), F32),
            jax.ShapeDtypeStruct((ranks, width), F32),
        ),
        in_specs=[smem()] + [vmem()] * 3,
        out_specs=(vmem(), vmem(), vmem()),
        scratch_shapes=[
            pltpu.VMEM((2, ranks, depth), BF16),
            pltpu.VMEM((ranks, width), BF16),
        ],
        name="outputs",
    )(adapter_ids, att, grad, raised)


def solution(mesh):
    in_specs = (
        P("row", None),
        P("row", None),
        P("pre", None),
        P("pre", None),
        P(None, "pre"),
        P(),
        P("row", None),
        P(),
        P("row", None),
    )
    out_specs = (P("row", None), P("row", None), P())
    body = functools.partial(shards, mesh.shape["pre"], mesh.shape["row"])
    return jax.shard_map(body, mesh=mesh, in_specs=in_specs, out_specs=out_specs, check_vma=False)
```

```python
import functools
import math

import jax
import jax.numpy as jnp
from jax import lax
from jax.experimental import pallas as pl
from jax.experimental.pallas import tpu as pltpu
from jax.sharding import PartitionSpec as P

HD = 128
RANK = 16
MB = 128
ADAPTER_SCALE = 2.0
DEAD = -1e30
FLOOR = -1e29
TINY = 1e-30
STEP = 512
LOG2E = math.log2(math.e)
MESH = pl.DeviceIdType.MESH
F32 = jnp.float32
BF16 = jnp.bfloat16


def dot(a, b, ca, cb):
    return lax.dot_general(a, b, (((ca,), (cb,)), ((), ())), preferred_element_type=F32)


def remote(src, dst, send_sem, recv_sem, pre, row):
    return pltpu.make_async_remote_copy(
        src_ref=src,
        dst_ref=dst,
        send_sem=send_sem,
        recv_sem=recv_sem,
        device_id=(pre, row),
        device_id_type=MESH,
    )


def plane_offsets(row_count):
    extent = (4, 4, 2) if row_count == 32 else (1, row_count // 2, 2)
    around = lambda n, size: min(n, size - n)
    offsets = [
        (around(x, extent[0]) + around(y, extent[1]), x, y, c)
        for x in range(extent[0])
        for y in range(extent[1])
        for c in range(extent[2])
    ]
    return extent, [o[1:] for o in sorted(offsets, key=lambda o: -o[0]) if o[1:] != (0, 0, 0)]


def plane_peer(row, extent, offset):
    _, ys, cs = extent
    x = (row // (ys * cs) + offset[0]) % extent[0]
    y = (row // cs % ys + offset[1]) % ys
    return (x * ys + y) * cs + (row % cs + offset[2]) % cs


def line_offsets(count):
    return sorted(range(1, count), key=lambda k: -min(k, count - k))


def picker(ids_ref, students, ranks):
    place = lax.broadcasted_iota(jnp.int32, (ranks, ranks), 0)
    column = lax.broadcasted_iota(jnp.int32, (ranks, ranks), 1)
    wanted = jnp.zeros((ranks, ranks), jnp.int32)
    for s in range(students):
        wanted = jnp.where(place // RANK == s, ids_ref[s] * RANK + place % RANK, wanted)
    return jnp.where(column == wanted, 1.0, 0.0).astype(BF16)


def query_kernel(
    per_student,
    row_count,
    ids_ref,
    a_hbm,
    hidden_hbm,
    up_hbm,
    base_hbm,
    latent_ref,
    query_ref,
    own_up_ref,
    outgoing,
    incoming,
    a_rows,
    hidden,
    up_rows,
    base_rows,
    send_sem,
    recv_sem,
    load_sem,
):
    pre = lax.axis_index("pre")
    row = lax.axis_index("row")
    students = row_count // per_student
    depth, ranks = a_hbm.shape
    barrier = pltpu.get_barrier_semaphore()

    def greet(k, carry):
        pl.semaphore_signal(
            barrier, inc=1, device_id=(pre, (row + k) % row_count), device_id_type=MESH
        )
        return carry

    lax.fori_loop(1, row_count, greet, 0)
    loads = [
        pltpu.make_async_copy(source, landing, load_sem.at[n])
        for n, (source, landing) in enumerate(
            ((a_hbm, a_rows), (hidden_hbm, hidden), (up_hbm, up_rows), (base_hbm, base_rows))
        )
    ]
    for copy in loads:
        copy.start()
    pick = picker(ids_ref, students, ranks)
    loads[0].wait()
    picked = dot(pick, a_rows[...], 1, 1).astype(BF16)
    for s in range(students):
        outgoing[s] = picked[s * RANK : (s + 1) * RANK]
    pl.semaphore_wait(barrier, row_count - 1)

    extent, offsets = plane_offsets(row_count)
    own_cols = pl.ds(pl.multiple_of(row * depth, depth), depth)
    copies = []
    for k, offset in enumerate(offsets):
        to = plane_peer(row, extent, offset)
        copies.append(
            remote(
                outgoing.at[to // per_student],
                incoming.at[:, own_cols],
                send_sem.at[k],
                recv_sem.at[row],
                pre,
                to,
            )
        )
        copies[-1].start()
    mine = row // per_student
    incoming[:, own_cols] = outgoing[mine]
    place = lax.broadcasted_iota(jnp.int32, (RANK, ranks), 0)
    column = lax.broadcasted_iota(jnp.int32, (RANK, ranks), 1)
    own_pick = jnp.where(column == ids_ref[mine] * RANK + place, 1.0, 0.0).astype(BF16)
    for copy in loads[1:]:
        copy.wait()
    up = dot(own_pick, up_rows[...], 1, 0).astype(BF16)
    own_up_ref[...] = up

    def take(k, carry):
        source = (row + k) % row_count
        cols = pl.ds(pl.multiple_of(source * depth, depth), depth)
        remote(
            outgoing.at[0], incoming.at[:, cols], send_sem.at[0], recv_sem.at[source], pre, row
        ).wait_recv()
        return carry

    lax.fori_loop(1, row_count, take, 0)
    total = dot(incoming[...], hidden[...], 1, 1)
    latent = total.astype(BF16)
    latent_ref[...] = latent
    raised = dot(latent, up, 0, 0)
    query_ref[...] = (base_rows[...].astype(F32) + ADAPTER_SCALE * raised).astype(BF16)

    for copy in copies:
        copy.wait_send()


def split_parts(x, count):
    parts = []
    for _ in range(count):
        part = x.astype(BF16).astype(F32)
        parts.append(part)
        x = x - part
    return parts


def attention_kernel(
    pre_count,
    row_count,
    per_student,
    mask_ref,
    query_hbm,
    upstream_hbm,
    key_hbm,
    value_hbm,
    latent_ref,
    up_ref,
    hidden_hbm,
    attended_ref,
    grad_ref,
    raised_ref,
    hidden,
    q_rows,
    u_rows,
    bias,
    value_key,
    weights,
    high_rows,
    delta_rows,
    sum_rows,
    both_rows,
    back_rows,
    part,
    stat,
    stat_out,
    stat_in,
    chain_out,
    chain_in,
    odd_out,
    odd_in,
    term_out,
    term_in,
    att_in,
    quarter_out,
    quarter_in,
    lift_out,
    lift_in,
    grad_out,
    grad_in,
    up_out,
    up_in,
    raised,
    load_sem,
    input_sem,
    stat_send,
    stat_recv,
    chain_send,
    chain_recv,
    odd_send,
    odd_recv,
    term_send,
    term_recv,
    att_send,
    att_recv,
    quarter_send,
    quarter_recv,
    lift_send,
    lift_recv,
    grad_send,
    grad_recv,
    up_send,
    up_recv,
):
    pre = lax.axis_index("pre")
    row = lax.axis_index("row")
    tokens = query_hbm.shape[0]
    heads = query_hbm.shape[1] // HD
    keys = key_hbm.shape[0]
    own_rows = heads * tokens // pre_count
    half = pre_count // 2
    steps = half // 2
    score_scale = 1.0 / math.sqrt(HD)
    fold = score_scale * LOG2E
    student = row // per_student
    place = row % per_student
    first_row = student * per_student
    depth = grad_out.shape[2]
    width = heads * HD // per_student
    extent, plane = plane_offsets(row_count)
    line = line_offsets(pre_count)
    barrier = pltpu.get_barrier_semaphore()

    loads = [
        pltpu.make_async_copy(key_hbm, value_key.at[:, HD:], input_sem.at[0]),
        pltpu.make_async_copy(value_hbm, value_key.at[:, :HD], input_sem.at[1]),
    ]
    for n, (source, landing) in enumerate(((query_hbm, q_rows), (upstream_hbm, u_rows))):
        for h in range(heads):
            loads.append(
                pltpu.make_async_copy(
                    source.at[:, h * HD : (h + 1) * HD],
                    landing.at[h * tokens : (h + 1) * tokens, :],
                    input_sem.at[2 + n * heads + h],
                )
            )
    for copy in loads:
        copy.start()
    load = pltpu.make_async_copy(hidden_hbm, hidden, load_sem)
    load.start()
    for k in line:
        pl.semaphore_signal(
            barrier, inc=1, device_id=((pre + k) % pre_count, row), device_id_type=MESH
        )
    for offset in plane:
        pl.semaphore_signal(
            barrier, inc=1, device_id=(pre, plane_peer(row, extent, offset)), device_id_type=MESH
        )

    for b in range(keys // MB):
        read = jnp.full((8, MB), mask_ref[student, b], jnp.int32)
        bias[:, b * MB : (b + 1) * MB] = jnp.where(read > 0, 0.0, DEAD)
    rows_all = heads * tokens
    step = weights.shape[2]
    lane = lax.broadcasted_iota(jnp.int32, (tokens, HD), 1)
    high_rows[...] = jnp.full((rows_all, HD), FLOOR, F32)
    for copy in loads:
        copy.wait()

    def score(j, carry):
        cols = pl.ds(pl.multiple_of(j * step, step), step)
        s = dot(q_rows[...], value_key[cols, HD:], 1, 1) + bias[0:1, cols]
        weights[j] = s
        high = high_rows[...]
        for g in range(step // HD):
            high = jnp.maximum(high, s[:, g * HD : (g + 1) * HD])
        high_rows[...] = high
        return carry

    lax.fori_loop(0, keys // step, score, 0)
    top = jnp.max(high_rows[...], axis=1, keepdims=True) * fold
    high_rows[...] = jnp.broadcast_to(top, (rows_all, HD))
    sum_rows[...] = jnp.zeros((rows_all, HD), F32)
    both_rows[...] = jnp.zeros((rows_all, 2 * HD), F32)

    def weigh(j, carry):
        cols = pl.ds(pl.multiple_of(j * step, step), step)
        level = high_rows[...]
        sums = sum_rows[...]
        ws = []
        for g in range(step // HD):
            w = jnp.exp2(weights[j, :, g * HD : (g + 1) * HD] * fold - level)
            weights[j, :, g * HD : (g + 1) * HD] = w
            sums = sums + w
            ws.append(w.astype(BF16))
        sum_rows[...] = sums
        both_rows[...] += dot(jnp.concatenate(ws, axis=1), value_key[cols, :], 1, 0)
        return carry

    lax.fori_loop(0, keys // step, weigh, 0)
    table = jnp.zeros((tokens, HD), F32)
    for h in range(heads):
        rows = slice(h * tokens, (h + 1) * tokens)
        l = jnp.maximum(jnp.sum(sum_rows[rows, :], axis=1, keepdims=True), TINY)
        weighed = u_rows[rows, :].astype(F32) * both_rows[rows, :HD]
        d = jnp.sum(weighed, axis=1, keepdims=True) / l
        lse = high_rows[rows, :] + jnp.log(l) * LOG2E
        delta_rows[rows, :] = jnp.broadcast_to(d, (tokens, HD))
        table = jnp.where(lane == h, lse, table)
        table = jnp.where(lane == heads + h, d, table)
    stat[...] = table

    stat_out[...] = stat[...].T[: 2 * heads]
    stat_in[pre] = stat_out[...]
    pl.semaphore_wait(barrier, row_count - 1 + pre_count - 1)

    def line_copies(source, landing, send_sem, recv_sem):
        return [
            remote(
                source,
                landing.at[pre],
                send_sem.at[n],
                recv_sem.at[pre],
                (pre + k) % pre_count,
                row,
            )
            for n, k in enumerate(line)
        ]

    def take_line(source, landing, send_sem, recv_sem):
        for k in reversed(line):
            origin = (pre + k) % pre_count
            remote(
                source, landing.at[origin], send_sem.at[0], recv_sem.at[origin], pre, row
            ).wait_recv()

    stat_copies = line_copies(stat_out, stat_in, stat_send, stat_recv)
    for copy in stat_copies:
        copy.start()

    back_rows[...] = jnp.zeros((rows_all, HD), F32)

    def backward(j, carry):
        cols = pl.ds(pl.multiple_of(j * step, step), step)
        dp = dot(u_rows[...], value_key[cols, :HD], 1, 1)
        d = delta_rows[...]
        g = [
            (weights[j, :, n * HD : (n + 1) * HD] * (dp[:, n * HD : (n + 1) * HD] - d)).astype(BF16)
            for n in range(step // HD)
        ]
        back_rows[...] += dot(jnp.concatenate(g, axis=1), value_key[cols, HD:], 1, 0)
        return carry

    lax.fori_loop(0, keys // step, backward, 0)

    take_line(stat_out, stat_in, stat_send, stat_recv)
    top = stat_in[0, :heads]
    for n in range(1, pre_count):
        top = jnp.maximum(top, stat_in[n, :heads])
    mass = jnp.zeros((heads, tokens), F32)
    mean = jnp.zeros((heads, tokens), F32)
    for n in range(pre_count):
        share = jnp.exp2(stat_in[n, :heads] - top)
        mass = mass + share
        mean = mean + share * stat_in[n, heads:]
    stat[:heads, :] = top + jnp.log(mass) * LOG2E
    stat[heads : 2 * heads, :] = mean / mass
    table = stat[...].T
    for h in range(heads):
        rows = slice(h * tokens, (h + 1) * tokens)
        factor = jnp.exp2(high_rows[rows, :] - table[:, h : h + 1])
        high_rows[rows, :] = factor
        part[rows, :] = both_rows[rows, :HD] * factor

    def hop(flow, distance):
        return (pre + (distance if flow == 0 else pre_count - distance)) % pre_count

    def own_part(flow, distance):
        chunk = hop(flow, distance)
        return part[pl.ds(pl.multiple_of(chunk * own_rows, own_rows), own_rows), :]

    def chain_copy(flow, t):
        return remote(
            chain_out.at[flow, t],
            chain_in.at[flow, t],
            chain_send.at[flow, t],
            chain_recv.at[flow, t],
            hop(flow, 2),
            row,
        )

    def odd_copy(flow, t):
        return remote(
            odd_out.at[flow, t],
            odd_in.at[flow, t],
            odd_send.at[flow, t],
            odd_recv.at[flow, t],
            hop(flow, 1),
            row,
        )

    sent = []

    def arrivals(flow, t, total):
        odd_copy(flow, t).wait_recv()
        total = total + odd_in[flow, t].astype(F32)
        if flow == 1 or t > 0:
            chain_copy(flow, t).wait_recv()
            total = total + chain_in[flow, t].astype(F32)
        return total

    def relay(t):
        for flow in (1, 0):
            total = arrivals(flow, t - 1, own_part(flow, half - 2 * t))
            chain_out[flow, t] = total.astype(BF16)
            sent.append(chain_copy(flow, t))
            sent[-1].start()

    chain_out[1, 0] = own_part(1, half).astype(BF16)
    sent.append(chain_copy(1, 0))
    sent[-1].start()
    for t in range(steps):
        for flow in (0, 1):
            odd_out[flow, t] = own_part(flow, half - 1 - 2 * t).astype(BF16)
            sent.append(odd_copy(flow, t))
            sent[-1].start()

    code = jnp.zeros((RANK, tokens), F32)
    for h in range(heads):
        rows = slice(h * tokens, (h + 1) * tokens)
        cols = slice(h * HD, (h + 1) * HD)
        shift = delta_rows[rows, :] - table[:, heads + h : heads + h + 1]
        grad_q = (back_rows[rows, :] + shift * both_rows[rows, HD:]) * (high_rows[rows, :] * score_scale)
        grad_q = grad_q.astype(BF16)
        code = code + dot(up_ref[:, cols], grad_q, 1, 1)
        raised[:, cols] = ADAPTER_SCALE * dot(latent_ref[...], grad_q, 1, 0)
    term_out[...] = (ADAPTER_SCALE * code).astype(BF16)
    term_copies = line_copies(term_out, term_in, term_send, term_recv)
    for copy in term_copies:
        copy.start()
    term_in[pre] = term_out[...]
    for n in range(per_student):
        quarter_out[n] = raised[:, n * width : (n + 1) * width].astype(BF16)

    def quarter_copy(k):
        to = (place + k) % per_student
        return remote(
            quarter_out.at[to],
            quarter_in.at[place],
            quarter_send.at[k],
            quarter_recv.at[place],
            pre,
            first_row + to,
        )

    for k in range(1, per_student):
        quarter_copy(k).start()
    quarter_in[place] = quarter_out[place]
    if steps > 1:
        relay(1)

    for k in range(1, per_student):
        origin = (place + k) % per_student
        remote(
            quarter_out.at[0],
            quarter_in.at[origin],
            quarter_send.at[0],
            quarter_recv.at[origin],
            pre,
            row,
        ).wait_recv()
    summed = jnp.zeros((RANK, width), F32)
    for n in range(per_student):
        summed = summed + quarter_in[n].astype(F32)
    lift_out[...] = summed.astype(BF16)
    lift_copies = line_copies(lift_out, lift_in, lift_send, lift_recv)
    for copy in lift_copies:
        copy.start()
    lift_in[pre] = lift_out[...]
    if steps > 2:
        relay(2)

    load.wait()
    take_line(term_out, term_in, term_send, term_recv)
    code = term_in[0].astype(F32)
    for n in range(1, pre_count):
        code = code + term_in[n].astype(F32)
    code = code.astype(BF16)
    grad_copies = []
    for n, offset in enumerate(plane):
        to = plane_peer(row, extent, offset)
        cols = pl.ds(pl.multiple_of(to * depth, depth), depth)
        grad_out[to] = dot(code, hidden[:, cols], 1, 0).astype(BF16)
        grad_copies.append(
            remote(grad_out.at[to], grad_in.at[row], grad_send.at[n], grad_recv.at[row], pre, to)
        )
        grad_copies[-1].start()
    cols = pl.ds(pl.multiple_of(row * depth, depth), depth)
    grad_in[row] = dot(code, hidden[:, cols], 1, 0).astype(BF16)
    for t in range(3, steps):
        relay(t)

    total = own_part(0, 0)
    for flow in (0, 1):
        total = arrivals(flow, steps - 1, total)
    att_in[pre] = total.astype(BF16)

    stride = max(pre_count // 4, 1)
    far = [k for k in (2 * stride, stride, 3 * stride) if k < pre_count]
    near = [k if k <= stride // 2 else k - stride for k in range(1, stride)]

    def att_copy(slot, n, k):
        return remote(
            att_in.at[slot],
            att_in.at[slot],
            att_send.at[n],
            att_recv.at[slot],
            (pre + k + pre_count) % pre_count,
            row,
        )

    att_copies = [att_copy(pre, n, k) for n, k in enumerate(far)]
    for copy in att_copies:
        copy.start()

    take_line(lift_out, lift_in, lift_send, lift_recv)
    summed = lift_in[0].astype(F32)
    for n in range(1, pre_count):
        summed = summed + lift_in[n].astype(F32)
    up_out[...] = summed.astype(BF16)
    up_copies = []
    for n, offset in enumerate(plane):
        to = plane_peer(row, extent, offset)
        up_copies.append(
            remote(up_out, up_in.at[row], up_send.at[n], up_recv.at[row], pre, to)
        )
        up_copies[-1].start()
    up_in[row] = up_out[...]

    def slot_wait(landing, slot, send_sem, recv_sem):
        remote(
            landing.at[slot], landing.at[slot], send_sem.at[0], recv_sem.at[slot], pre, row
        ).wait_recv()

    for k in far:
        slot_wait(att_in, (pre + k) % pre_count, att_send, att_recv)
    for k in near:
        for n in range(len(far) + 1):
            slot = (pre + n * stride) % pre_count
            att_copies.append(att_copy(slot, len(att_copies), k))
            att_copies[-1].start()

    def take_grad(k, carry):
        slot_wait(grad_in, (row + k) % row_count, grad_send, grad_recv)
        return carry

    lax.fori_loop(1, row_count, take_grad, 0)
    grad_ref[...] = grad_in[...]
    for k in near:
        for n in range(len(far) + 1):
            slot = (pre - k + n * stride + pre_count) % pre_count
            slot_wait(att_in, slot, att_send, att_recv)
    attended_ref[...] = att_in[...]

    def take_up(k, carry):
        slot_wait(up_in, (row + k) % row_count, up_send, up_recv)
        return carry

    lax.fori_loop(1, row_count, take_up, 0)
    raised_ref[...] = up_in[...]

    for copy in stat_copies + sent + term_copies + lift_copies + att_copies + grad_copies + up_copies:
        copy.wait_send()
    for k in range(1, per_student):
        quarter_copy(k).wait_send()


def output_kernel(
    per_student, ids_ref, att_ref, grad_ref, raised_ref, attended_ref, grad_a_ref, grad_up_ref, rows, ups
):
    count, own_rows, _ = att_ref.shape
    tokens = attended_ref.shape[0]
    pieces = tokens // own_rows
    students = grad_ref.shape[0] // per_student
    width = raised_ref.shape[2]
    pick = picker(ids_ref, students, students * RANK)
    for s in range(students):
        block_sum = grad_ref[s * per_student].astype(F32)
        for n in range(1, per_student):
            block_sum = block_sum + grad_ref[s * per_student + n].astype(F32)
        for n, piece in enumerate(split_parts(block_sum, 2)):
            rows[n, s * RANK : (s + 1) * RANK, :] = piece.astype(BF16)
        for j in range(per_student):
            ups[s * RANK : (s + 1) * RANK, j * width : (j + 1) * width] = raised_ref[
                s * per_student + j
            ]
    grad_a_ref[...] = dot(rows[0], pick, 0, 0) + dot(rows[1], pick, 0, 0)
    grad_up_ref[...] = dot(pick, ups[...], 0, 0)
    for c in range(count):
        h, n = c // pieces, c % pieces
        attended_ref[n * own_rows : (n + 1) * own_rows, h * HD : (h + 1) * HD] = att_ref[c]


def vmem():
    return pl.BlockSpec(memory_space=pltpu.VMEM)


def smem():
    return pl.BlockSpec(memory_space=pltpu.SMEM)


def anywhere():
    return pl.BlockSpec(memory_space=pl.ANY)


def shards(
    pre_count,
    row_count,
    hidden_in,
    frozen_query_base,
    k_prefix,
    v_prefix,
    tree_mask,
    adapter_ids,
    a_down,
    up_weight_matrix,
    cotangent,
):
    tokens, width = frozen_query_base.shape
    model = hidden_in.shape[1]
    heads = width // HD
    keys = k_prefix.shape[0]
    depth, ranks = a_down.shape
    students = tree_mask.shape[0]
    per_student = row_count // students
    dma = pltpu.SemaphoreType.DMA
    latent, queries, own_up = pl.pallas_call(
        functools.partial(query_kernel, per_student, row_count),
        out_shape=(
            jax.ShapeDtypeStruct((RANK, tokens), BF16),
            jax.ShapeDtypeStruct((tokens, width), BF16),
            jax.ShapeDtypeStruct((RANK, width), BF16),
        ),
        in_specs=[smem()] + [anywhere()] * 4,
        out_specs=(vmem(), vmem(), vmem()),
        scratch_shapes=[
            pltpu.VMEM((students, RANK, depth), BF16),
            pltpu.VMEM((RANK, model), BF16),
            pltpu.VMEM((depth, ranks), BF16),
            pltpu.VMEM((tokens, model), BF16),
            pltpu.VMEM((ranks, width), BF16),
            pltpu.VMEM((tokens, width), BF16),
            dma((row_count,)),
            dma((row_count,)),
            dma((4,)),
        ],
        compiler_params=pltpu.CompilerParams(collective_id=0, has_side_effects=True),
        name="queries",
    )(adapter_ids, a_down, hidden_in, up_weight_matrix, frozen_query_base)

    rows = heads * tokens
    own_rows = rows // pre_count
    steps = pre_count // 4
    quarter = width // per_student
    ring = (2, steps)
    att, grad, raised = pl.pallas_call(
        functools.partial(attention_kernel, pre_count, row_count, per_student),
        out_shape=(
            jax.ShapeDtypeStruct((pre_count, own_rows, HD), BF16),
            jax.ShapeDtypeStruct((row_count, RANK, depth), BF16),
            jax.ShapeDtypeStruct((row_count, RANK, quarter), BF16),
        ),
        in_specs=[smem()] + [anywhere()] * 4 + [vmem()] * 2 + [anywhere()],
        out_specs=(vmem(), vmem(), vmem()),
        scratch_shapes=[
            pltpu.VMEM((tokens, model), BF16),
            pltpu.VMEM((rows, HD), BF16),
            pltpu.VMEM((rows, HD), BF16),
            pltpu.VMEM((8, keys), F32),
            pltpu.VMEM((keys, 2 * HD), BF16),
            pltpu.VMEM((keys // STEP, rows, STEP), F32),
            pltpu.VMEM((rows, HD), F32),
            pltpu.VMEM((rows, HD), F32),
            pltpu.VMEM((rows, HD), F32),
            pltpu.VMEM((rows, 2 * HD), F32),
            pltpu.VMEM((rows, HD), F32),
            pltpu.VMEM((rows, HD), F32),
            pltpu.VMEM((tokens, HD), F32),
            pltpu.VMEM((2 * heads, tokens), F32),
            pltpu.VMEM((pre_count, 2 * heads, tokens), F32),
            pltpu.VMEM(ring + (own_rows, HD), BF16),
            pltpu.VMEM(ring + (own_rows, HD), BF16),
            pltpu.VMEM(ring + (own_rows, HD), BF16),
            pltpu.VMEM(ring + (own_rows, HD), BF16),
            pltpu.VMEM((RANK, tokens), BF16),
            pltpu.VMEM((pre_count, RANK, tokens), BF16),
            pltpu.VMEM((pre_count, own_rows, HD), BF16),
            pltpu.VMEM((per_student, RANK, quarter), BF16),
            pltpu.VMEM((per_student, RANK, quarter), BF16),
            pltpu.VMEM((RANK, quarter), BF16),
            pltpu.VMEM((pre_count, RANK, quarter), BF16),
            pltpu.VMEM((row_count, RANK, depth), BF16),
            pltpu.VMEM((row_count, RANK, depth), BF16),
            pltpu.VMEM((RANK, quarter), BF16),
            pltpu.VMEM((row_count, RANK, quarter), BF16),
            pltpu.VMEM((RANK, width), F32),
            dma,
            dma((2 + 2 * heads,)),
            dma((pre_count,)),
            dma((pre_count,)),
            dma(ring),
            dma(ring),
            dma(ring),
            dma(ring),
            dma((pre_count,)),
            dma((pre_count,)),
            dma((pre_count,)),
            dma((pre_count,)),
            dma((per_student,)),
            dma((per_student,)),
            dma((pre_count,)),
            dma((pre_count,)),
            dma((row_count,)),
            dma((row_count,)),
            dma((row_count,)),
            dma((row_count,)),
        ],
        compiler_params=pltpu.CompilerParams(collective_id=1, has_side_effects=True),
        name="attention",
    )(tree_mask, queries, cotangent, k_prefix, v_prefix, latent, own_up, hidden_in)
    return pl.pallas_call(
        functools.partial(output_kernel, per_student),
        out_shape=(
            jax.ShapeDtypeStruct((tokens, width), BF16),
            jax.ShapeDtypeStruct((depth, ranks), F32),
            jax.ShapeDtypeStruct((ranks, width), F32),
        ),
        in_specs=[smem()] + [vmem()] * 3,
        out_specs=(vmem(), vmem(), vmem()),
        scratch_shapes=[
            pltpu.VMEM((2, ranks, depth), BF16),
            pltpu.VMEM((ranks, width), BF16),
        ],
        name="outputs",
    )(adapter_ids, att, grad, raised)


def solution(mesh):
    in_specs = (
        P("row", None),
        P("row", None),
        P("pre", None),
        P("pre", None),
        P(None, "pre"),
        P(),
        P("row", None),
        P(),
        P("row", None),
    )
    out_specs = (P("row", None), P("row", None), P())
    body = functools.partial(shards, mesh.shape["pre"], mesh.shape["row"])
    return jax.shard_map(body, mesh=mesh, in_specs=in_specs, out_specs=out_specs, check_vma=False)
```

```python
import functools
import math

import jax
import jax.numpy as jnp
from jax import lax
from jax.experimental import pallas as pl
from jax.experimental.pallas import tpu as pltpu
from jax.sharding import PartitionSpec as P

HD = 128
RANK = 16
MB = 128
ADAPTER_SCALE = 2.0
DEAD = -1e30
FLOOR = -1e29
TINY = 1e-30
STEP = 512
LOG2E = math.log2(math.e)
MESH = pl.DeviceIdType.MESH
F32 = jnp.float32
BF16 = jnp.bfloat16


def dot(a, b, ca, cb):
    return lax.dot_general(a, b, (((ca,), (cb,)), ((), ())), preferred_element_type=F32)


def remote(src, dst, send_sem, recv_sem, pre, row):
    return pltpu.make_async_remote_copy(
        src_ref=src,
        dst_ref=dst,
        send_sem=send_sem,
        recv_sem=recv_sem,
        device_id=(pre, row),
        device_id_type=MESH,
    )


def plane_offsets(row_count):
    extent = (4, 4, 2) if row_count == 32 else (1, row_count // 2, 2)
    around = lambda n, size: min(n, size - n)
    offsets = [
        (around(x, extent[0]) + around(y, extent[1]), x, y, c)
        for x in range(extent[0])
        for y in range(extent[1])
        for c in range(extent[2])
    ]
    return extent, [o[1:] for o in sorted(offsets, key=lambda o: -o[0]) if o[1:] != (0, 0, 0)]


def plane_peer(row, extent, offset):
    _, ys, cs = extent
    x = (row // (ys * cs) + offset[0]) % extent[0]
    y = (row // cs % ys + offset[1]) % ys
    return (x * ys + y) * cs + (row % cs + offset[2]) % cs


def line_offsets(count):
    return sorted(range(1, count), key=lambda k: -min(k, count - k))


def picker(ids_ref, students, ranks):
    place = lax.broadcasted_iota(jnp.int32, (ranks, ranks), 0)
    column = lax.broadcasted_iota(jnp.int32, (ranks, ranks), 1)
    wanted = jnp.zeros((ranks, ranks), jnp.int32)
    for s in range(students):
        wanted = jnp.where(place // RANK == s, ids_ref[s] * RANK + place % RANK, wanted)
    return jnp.where(column == wanted, 1.0, 0.0).astype(BF16)


def query_kernel(
    per_student,
    row_count,
    ids_ref,
    a_hbm,
    hidden_hbm,
    up_hbm,
    base_hbm,
    latent_ref,
    query_ref,
    own_up_ref,
    outgoing,
    incoming,
    a_rows,
    hidden,
    up_rows,
    base_rows,
    send_sem,
    recv_sem,
    load_sem,
):
    pre = lax.axis_index("pre")
    row = lax.axis_index("row")
    students = row_count // per_student
    depth, ranks = a_hbm.shape
    barrier = pltpu.get_barrier_semaphore()

    def greet(k, carry):
        pl.semaphore_signal(
            barrier, inc=1, device_id=(pre, (row + k) % row_count), device_id_type=MESH
        )
        return carry

    lax.fori_loop(1, row_count, greet, 0)
    loads = [
        pltpu.make_async_copy(source, landing, load_sem.at[n])
        for n, (source, landing) in enumerate(
            ((a_hbm, a_rows), (hidden_hbm, hidden), (up_hbm, up_rows), (base_hbm, base_rows))
        )
    ]
    for copy in loads:
        copy.start()
    pick = picker(ids_ref, students, ranks)
    loads[0].wait()
    picked = dot(pick, a_rows[...], 1, 1).astype(BF16)
    for s in range(students):
        outgoing[s] = picked[s * RANK : (s + 1) * RANK]
    pl.semaphore_wait(barrier, row_count - 1)

    extent, offsets = plane_offsets(row_count)
    own_cols = pl.ds(pl.multiple_of(row * depth, depth), depth)
    copies = []
    for k, offset in enumerate(offsets):
        to = plane_peer(row, extent, offset)
        copies.append(
            remote(
                outgoing.at[to // per_student],
                incoming.at[:, own_cols],
                send_sem.at[k],
                recv_sem.at[row],
                pre,
                to,
            )
        )
        copies[-1].start()
    mine = row // per_student
    incoming[:, own_cols] = outgoing[mine]
    place = lax.broadcasted_iota(jnp.int32, (RANK, ranks), 0)
    column = lax.broadcasted_iota(jnp.int32, (RANK, ranks), 1)
    own_pick = jnp.where(column == ids_ref[mine] * RANK + place, 1.0, 0.0).astype(BF16)
    for copy in loads[1:]:
        copy.wait()
    up = dot(own_pick, up_rows[...], 1, 0).astype(BF16)
    own_up_ref[...] = up

    def take(k, carry):
        source = (row + k) % row_count
        cols = pl.ds(pl.multiple_of(source * depth, depth), depth)
        remote(
            outgoing.at[0], incoming.at[:, cols], send_sem.at[0], recv_sem.at[source], pre, row
        ).wait_recv()
        return carry

    lax.fori_loop(1, row_count, take, 0)
    total = dot(incoming[...], hidden[...], 1, 1)
    latent = total.astype(BF16)
    latent_ref[...] = latent
    raised = dot(latent, up, 0, 0)
    query_ref[...] = (base_rows[...].astype(F32) + ADAPTER_SCALE * raised).astype(BF16)

    for copy in copies:
        copy.wait_send()


def split_parts(x, count):
    parts = []
    for _ in range(count):
        part = x.astype(BF16).astype(F32)
        parts.append(part)
        x = x - part
    return parts


def attention_kernel(
    pre_count,
    row_count,
    per_student,
    mask_ref,
    query_hbm,
    upstream_hbm,
    key_hbm,
    value_hbm,
    latent_ref,
    up_ref,
    hidden_hbm,
    attended_ref,
    grad_ref,
    raised_ref,
    hidden,
    q_rows,
    u_rows,
    bias,
    value_key,
    weights,
    high_rows,
    delta_rows,
    sum_rows,
    both_rows,
    back_rows,
    part,
    stat,
    stat_out,
    stat_in,
    sum_out,
    sum_in,
    term_out,
    term_in,
    att_in,
    quarter_out,
    quarter_in,
    lift_out,
    lift_in,
    grad_out,
    grad_in,
    up_out,
    up_in,
    raised,
    load_sem,
    input_sem,
    stat_send,
    stat_recv,
    sum_send,
    sum_recv,
    term_send,
    term_recv,
    att_send,
    att_recv,
    quarter_send,
    quarter_recv,
    lift_send,
    lift_recv,
    grad_send,
    grad_recv,
    up_send,
    up_recv,
):
    pre = lax.axis_index("pre")
    row = lax.axis_index("row")
    tokens = query_hbm.shape[0]
    heads = query_hbm.shape[1] // HD
    keys = key_hbm.shape[0]
    own_rows = heads * tokens // pre_count
    half = pre_count // 2
    stride = half // 2
    score_scale = 1.0 / math.sqrt(HD)
    fold = score_scale * LOG2E
    student = row // per_student
    place = row % per_student
    first_row = student * per_student
    depth = grad_out.shape[2]
    width = heads * HD // per_student
    extent, plane = plane_offsets(row_count)
    line = line_offsets(pre_count)
    barrier = pltpu.get_barrier_semaphore()

    loads = [
        pltpu.make_async_copy(key_hbm, value_key.at[:, HD:], input_sem.at[0]),
        pltpu.make_async_copy(value_hbm, value_key.at[:, :HD], input_sem.at[1]),
    ]
    for n, (source, landing) in enumerate(((query_hbm, q_rows), (upstream_hbm, u_rows))):
        for h in range(heads):
            loads.append(
                pltpu.make_async_copy(
                    source.at[:, h * HD : (h + 1) * HD],
                    landing.at[h * tokens : (h + 1) * tokens, :],
                    input_sem.at[2 + n * heads + h],
                )
            )
    for copy in loads:
        copy.start()
    load = pltpu.make_async_copy(hidden_hbm, hidden, load_sem)
    load.start()
    for k in line:
        pl.semaphore_signal(
            barrier, inc=1, device_id=((pre + k) % pre_count, row), device_id_type=MESH
        )
    for offset in plane:
        pl.semaphore_signal(
            barrier, inc=1, device_id=(pre, plane_peer(row, extent, offset)), device_id_type=MESH
        )

    for b in range(keys // MB):
        read = jnp.full((8, MB), mask_ref[student, b], jnp.int32)
        bias[:, b * MB : (b + 1) * MB] = jnp.where(read > 0, 0.0, DEAD)
    rows_all = heads * tokens
    step = weights.shape[2]
    lane = lax.broadcasted_iota(jnp.int32, (tokens, HD), 1)
    high_rows[...] = jnp.full((rows_all, HD), FLOOR, F32)
    for copy in loads:
        copy.wait()

    def score(j, carry):
        cols = pl.ds(pl.multiple_of(j * step, step), step)
        s = dot(q_rows[...], value_key[cols, HD:], 1, 1) + bias[0:1, cols]
        weights[j] = s
        high = high_rows[...]
        for g in range(step // HD):
            high = jnp.maximum(high, s[:, g * HD : (g + 1) * HD])
        high_rows[...] = high
        return carry

    lax.fori_loop(0, keys // step, score, 0)
    top = jnp.max(high_rows[...], axis=1, keepdims=True) * fold
    high_rows[...] = jnp.broadcast_to(top, (rows_all, HD))
    sum_rows[...] = jnp.zeros((rows_all, HD), F32)
    both_rows[...] = jnp.zeros((rows_all, 2 * HD), F32)

    def weigh(j, carry):
        cols = pl.ds(pl.multiple_of(j * step, step), step)
        level = high_rows[...]
        sums = sum_rows[...]
        ws = []
        for g in range(step // HD):
            w = jnp.exp2(weights[j, :, g * HD : (g + 1) * HD] * fold - level)
            weights[j, :, g * HD : (g + 1) * HD] = w
            sums = sums + w
            ws.append(w.astype(BF16))
        sum_rows[...] = sums
        both_rows[...] += dot(jnp.concatenate(ws, axis=1), value_key[cols, :], 1, 0)
        return carry

    lax.fori_loop(0, keys // step, weigh, 0)
    table = jnp.zeros((tokens, HD), F32)
    for h in range(heads):
        rows = slice(h * tokens, (h + 1) * tokens)
        l = jnp.maximum(jnp.sum(sum_rows[rows, :], axis=1, keepdims=True), TINY)
        weighed = u_rows[rows, :].astype(F32) * both_rows[rows, :HD]
        d = jnp.sum(weighed, axis=1, keepdims=True) / l
        lse = high_rows[rows, :] + jnp.log(l) * LOG2E
        delta_rows[rows, :] = jnp.broadcast_to(d, (tokens, HD))
        table = jnp.where(lane == h, lse, table)
        table = jnp.where(lane == heads + h, d, table)
    stat[...] = table

    stat_out[...] = stat[...].T[: 2 * heads]
    stat_in[pre] = stat_out[...]
    pl.semaphore_wait(barrier, row_count - 1 + pre_count - 1)

    def line_copies(source, landing, send_sem, recv_sem):
        return [
            remote(
                source,
                landing.at[pre],
                send_sem.at[n],
                recv_sem.at[pre],
                (pre + k) % pre_count,
                row,
            )
            for n, k in enumerate(line)
        ]

    def take_line(source, landing, send_sem, recv_sem):
        for k in reversed(line):
            origin = (pre + k) % pre_count
            remote(
                source, landing.at[origin], send_sem.at[0], recv_sem.at[origin], pre, row
            ).wait_recv()

    stat_copies = line_copies(stat_out, stat_in, stat_send, stat_recv)
    for copy in stat_copies:
        copy.start()

    back_rows[...] = jnp.zeros((rows_all, HD), F32)

    def backward(j, carry):
        cols = pl.ds(pl.multiple_of(j * step, step), step)
        dp = dot(u_rows[...], value_key[cols, :HD], 1, 1)
        d = delta_rows[...]
        g = [
            (weights[j, :, n * HD : (n + 1) * HD] * (dp[:, n * HD : (n + 1) * HD] - d)).astype(BF16)
            for n in range(step // HD)
        ]
        back_rows[...] += dot(jnp.concatenate(g, axis=1), value_key[cols, HD:], 1, 0)
        return carry

    lax.fori_loop(0, keys // step, backward, 0)

    take_line(stat_out, stat_in, stat_send, stat_recv)
    top = stat_in[0, :heads]
    for n in range(1, pre_count):
        top = jnp.maximum(top, stat_in[n, :heads])
    mass = jnp.zeros((heads, tokens), F32)
    mean = jnp.zeros((heads, tokens), F32)
    for n in range(pre_count):
        share = jnp.exp2(stat_in[n, :heads] - top)
        mass = mass + share
        mean = mean + share * stat_in[n, heads:]
    stat[:heads, :] = top + jnp.log(mass) * LOG2E
    stat[heads : 2 * heads, :] = mean / mass
    table = stat[...].T
    for h in range(heads):
        rows = slice(h * tokens, (h + 1) * tokens)
        factor = jnp.exp2(high_rows[rows, :] - table[:, h : h + 1])
        high_rows[rows, :] = factor
        part[rows, :] = both_rows[rows, :HD] * factor

    def hop(flow, distance):
        return (pre + (distance if flow == 0 else pre_count - distance)) % pre_count

    def own_part(flow, distance):
        chunk = hop(flow, distance)
        return part[pl.ds(pl.multiple_of(chunk * own_rows, own_rows), own_rows), :]

    def sum_copy(flow, distance):
        return remote(
            sum_out.at[flow, distance],
            sum_in.at[flow, distance],
            sum_send.at[flow, distance],
            sum_recv.at[flow, distance],
            hop(flow, distance if distance <= stride else distance - stride),
            row,
        )

    def reach(flow):
        return half - 1 + flow

    sent = []

    def send_sum(flow, distance, total):
        sum_out[flow, distance] = total.astype(BF16)
        sent.append(sum_copy(flow, distance))
        sent[-1].start()

    def arrivals(flow, distances, total):
        for distance in distances:
            sum_copy(flow, distance).wait_recv()
            total = total + sum_in[flow, distance].astype(F32)
        return total

    for distance in range(half, stride, -1):
        for flow in (1, 0):
            if distance <= reach(flow):
                send_sum(flow, distance, own_part(flow, distance))
    for distance in range(stride - 1, 0, -1):
        for flow in (1, 0):
            send_sum(flow, distance, own_part(flow, distance))

    code = jnp.zeros((RANK, tokens), F32)
    for h in range(heads):
        rows = slice(h * tokens, (h + 1) * tokens)
        cols = slice(h * HD, (h + 1) * HD)
        shift = delta_rows[rows, :] - table[:, heads + h : heads + h + 1]
        grad_q = (back_rows[rows, :] + shift * both_rows[rows, HD:]) * (high_rows[rows, :] * score_scale)
        grad_q = grad_q.astype(BF16)
        code = code + dot(up_ref[:, cols], grad_q, 1, 1)
        raised[:, cols] = ADAPTER_SCALE * dot(latent_ref[...], grad_q, 1, 0)
    term_out[...] = (ADAPTER_SCALE * code).astype(BF16)
    term_copies = line_copies(term_out, term_in, term_send, term_recv)
    for copy in term_copies:
        copy.start()
    term_in[pre] = term_out[...]
    for n in range(per_student):
        quarter_out[n] = raised[:, n * width : (n + 1) * width].astype(BF16)

    def quarter_copy(k):
        to = (place + k) % per_student
        return remote(
            quarter_out.at[to],
            quarter_in.at[place],
            quarter_send.at[k],
            quarter_recv.at[place],
            pre,
            first_row + to,
        )

    for k in range(1, per_student):
        quarter_copy(k).start()
    quarter_in[place] = quarter_out[place]

    for k in range(1, per_student):
        origin = (place + k) % per_student
        remote(
            quarter_out.at[0],
            quarter_in.at[origin],
            quarter_send.at[0],
            quarter_recv.at[origin],
            pre,
            row,
        ).wait_recv()
    summed = jnp.zeros((RANK, width), F32)
    for n in range(per_student):
        summed = summed + quarter_in[n].astype(F32)
    lift_out[...] = summed.astype(BF16)
    lift_copies = line_copies(lift_out, lift_in, lift_send, lift_recv)
    for copy in lift_copies:
        copy.start()
    lift_in[pre] = lift_out[...]
    for flow in (1, 0):
        beyond = range(stride + 1, reach(flow) + 1)
        send_sum(flow, stride, arrivals(flow, beyond, own_part(flow, stride)))

    load.wait()
    take_line(term_out, term_in, term_send, term_recv)
    code = term_in[0].astype(F32)
    for n in range(1, pre_count):
        code = code + term_in[n].astype(F32)
    code = code.astype(BF16)
    grad_copies = []
    for n, offset in enumerate(plane):
        to = plane_peer(row, extent, offset)
        cols = pl.ds(pl.multiple_of(to * depth, depth), depth)
        grad_out[to] = dot(code, hidden[:, cols], 1, 0).astype(BF16)
        grad_copies.append(
            remote(grad_out.at[to], grad_in.at[row], grad_send.at[n], grad_recv.at[row], pre, to)
        )
        grad_copies[-1].start()
    cols = pl.ds(pl.multiple_of(row * depth, depth), depth)
    grad_in[row] = dot(code, hidden[:, cols], 1, 0).astype(BF16)

    total = own_part(0, 0)
    for flow in (0, 1):
        total = arrivals(flow, range(1, stride + 1), total)
    att_in[pre] = total.astype(BF16)
    att_copies = []

    def give(slot, flow, distance):
        n = len(att_copies)
        att_copies.append(
            remote(
                att_in.at[slot],
                att_in.at[slot],
                att_send.at[n],
                att_recv.at[slot],
                hop(flow, distance),
                row,
            )
        )
        att_copies[-1].start()

    for distance in range(stride, 0, -1):
        for flow in (1, 0):
            give(pre, flow, distance)

    take_line(lift_out, lift_in, lift_send, lift_recv)
    summed = lift_in[0].astype(F32)
    for n in range(1, pre_count):
        summed = summed + lift_in[n].astype(F32)
    up_out[...] = summed.astype(BF16)
    up_copies = []
    for n, offset in enumerate(plane):
        to = plane_peer(row, extent, offset)
        up_copies.append(
            remote(up_out, up_in.at[row], up_send.at[n], up_recv.at[row], pre, to)
        )
        up_copies[-1].start()
    up_in[row] = up_out[...]

    def slot_wait(landing, slot, send_sem, recv_sem):
        remote(
            landing.at[slot], landing.at[slot], send_sem.at[0], recv_sem.at[slot], pre, row
        ).wait_recv()

    for flow in (1, 0):
        behind = hop(1 - flow, stride)
        slot_wait(att_in, behind, att_send, att_recv)
        for distance in range(reach(flow) - stride, 0, -1):
            give(behind, flow, distance)

    def take_grad(k, carry):
        slot_wait(grad_in, (row + k) % row_count, grad_send, grad_recv)
        return carry

    lax.fori_loop(1, row_count, take_grad, 0)
    grad_ref[...] = grad_in[...]
    for k in range(1, pre_count):
        if k not in (stride, pre_count - stride):
            slot_wait(att_in, (pre + k) % pre_count, att_send, att_recv)
    attended_ref[...] = att_in[...]

    def take_up(k, carry):
        slot_wait(up_in, (row + k) % row_count, up_send, up_recv)
        return carry

    lax.fori_loop(1, row_count, take_up, 0)
    raised_ref[...] = up_in[...]

    for copy in stat_copies + sent + term_copies + lift_copies + att_copies + grad_copies + up_copies:
        copy.wait_send()
    for k in range(1, per_student):
        quarter_copy(k).wait_send()


def output_kernel(
    per_student, ids_ref, att_ref, grad_ref, raised_ref, attended_ref, grad_a_ref, grad_up_ref, rows, ups
):
    count, own_rows, _ = att_ref.shape
    tokens = attended_ref.shape[0]
    pieces = tokens // own_rows
    students = grad_ref.shape[0] // per_student
    width = raised_ref.shape[2]
    pick = picker(ids_ref, students, students * RANK)
    for s in range(students):
        block_sum = grad_ref[s * per_student].astype(F32)
        for n in range(1, per_student):
            block_sum = block_sum + grad_ref[s * per_student + n].astype(F32)
        for n, piece in enumerate(split_parts(block_sum, 2)):
            rows[n, s * RANK : (s + 1) * RANK, :] = piece.astype(BF16)
        for j in range(per_student):
            ups[s * RANK : (s + 1) * RANK, j * width : (j + 1) * width] = raised_ref[
                s * per_student + j
            ]
    grad_a_ref[...] = dot(rows[0], pick, 0, 0) + dot(rows[1], pick, 0, 0)
    grad_up_ref[...] = dot(pick, ups[...], 0, 0)
    for c in range(count):
        h, n = c // pieces, c % pieces
        attended_ref[n * own_rows : (n + 1) * own_rows, h * HD : (h + 1) * HD] = att_ref[c]


def vmem():
    return pl.BlockSpec(memory_space=pltpu.VMEM)


def smem():
    return pl.BlockSpec(memory_space=pltpu.SMEM)


def anywhere():
    return pl.BlockSpec(memory_space=pl.ANY)


def shards(
    pre_count,
    row_count,
    hidden_in,
    frozen_query_base,
    k_prefix,
    v_prefix,
    tree_mask,
    adapter_ids,
    a_down,
    up_weight_matrix,
    cotangent,
):
    tokens, width = frozen_query_base.shape
    model = hidden_in.shape[1]
    heads = width // HD
    keys = k_prefix.shape[0]
    depth, ranks = a_down.shape
    students = tree_mask.shape[0]
    per_student = row_count // students
    dma = pltpu.SemaphoreType.DMA
    latent, queries, own_up = pl.pallas_call(
        functools.partial(query_kernel, per_student, row_count),
        out_shape=(
            jax.ShapeDtypeStruct((RANK, tokens), BF16),
            jax.ShapeDtypeStruct((tokens, width), BF16),
            jax.ShapeDtypeStruct((RANK, width), BF16),
        ),
        in_specs=[smem()] + [anywhere()] * 4,
        out_specs=(vmem(), vmem(), vmem()),
        scratch_shapes=[
            pltpu.VMEM((students, RANK, depth), BF16),
            pltpu.VMEM((RANK, model), BF16),
            pltpu.VMEM((depth, ranks), BF16),
            pltpu.VMEM((tokens, model), BF16),
            pltpu.VMEM((ranks, width), BF16),
            pltpu.VMEM((tokens, width), BF16),
            dma((row_count,)),
            dma((row_count,)),
            dma((4,)),
        ],
        compiler_params=pltpu.CompilerParams(collective_id=0, has_side_effects=True),
        name="queries",
    )(adapter_ids, a_down, hidden_in, up_weight_matrix, frozen_query_base)

    rows = heads * tokens
    own_rows = rows // pre_count
    quarter = width // per_student
    ring = (2, pre_count // 2 + 1)
    att, grad, raised = pl.pallas_call(
        functools.partial(attention_kernel, pre_count, row_count, per_student),
        out_shape=(
            jax.ShapeDtypeStruct((pre_count, own_rows, HD), BF16),
            jax.ShapeDtypeStruct((row_count, RANK, depth), BF16),
            jax.ShapeDtypeStruct((row_count, RANK, quarter), BF16),
        ),
        in_specs=[smem()] + [anywhere()] * 4 + [vmem()] * 2 + [anywhere()],
        out_specs=(vmem(), vmem(), vmem()),
        scratch_shapes=[
            pltpu.VMEM((tokens, model), BF16),
            pltpu.VMEM((rows, HD), BF16),
            pltpu.VMEM((rows, HD), BF16),
            pltpu.VMEM((8, keys), F32),
            pltpu.VMEM((keys, 2 * HD), BF16),
            pltpu.VMEM((keys // STEP, rows, STEP), F32),
            pltpu.VMEM((rows, HD), F32),
            pltpu.VMEM((rows, HD), F32),
            pltpu.VMEM((rows, HD), F32),
            pltpu.VMEM((rows, 2 * HD), F32),
            pltpu.VMEM((rows, HD), F32),
            pltpu.VMEM((rows, HD), F32),
            pltpu.VMEM((tokens, HD), F32),
            pltpu.VMEM((2 * heads, tokens), F32),
            pltpu.VMEM((pre_count, 2 * heads, tokens), F32),
            pltpu.VMEM(ring + (own_rows, HD), BF16),
            pltpu.VMEM(ring + (own_rows, HD), BF16),
            pltpu.VMEM((RANK, tokens), BF16),
            pltpu.VMEM((pre_count, RANK, tokens), BF16),
            pltpu.VMEM((pre_count, own_rows, HD), BF16),
            pltpu.VMEM((per_student, RANK, quarter), BF16),
            pltpu.VMEM((per_student, RANK, quarter), BF16),
            pltpu.VMEM((RANK, quarter), BF16),
            pltpu.VMEM((pre_count, RANK, quarter), BF16),
            pltpu.VMEM((row_count, RANK, depth), BF16),
            pltpu.VMEM((row_count, RANK, depth), BF16),
            pltpu.VMEM((RANK, quarter), BF16),
            pltpu.VMEM((row_count, RANK, quarter), BF16),
            pltpu.VMEM((RANK, width), F32),
            dma,
            dma((2 + 2 * heads,)),
            dma((pre_count,)),
            dma((pre_count,)),
            dma(ring),
            dma(ring),
            dma((pre_count,)),
            dma((pre_count,)),
            dma((pre_count,)),
            dma((pre_count,)),
            dma((per_student,)),
            dma((per_student,)),
            dma((pre_count,)),
            dma((pre_count,)),
            dma((row_count,)),
            dma((row_count,)),
            dma((row_count,)),
            dma((row_count,)),
        ],
        compiler_params=pltpu.CompilerParams(collective_id=1, has_side_effects=True),
        name="attention",
    )(tree_mask, queries, cotangent, k_prefix, v_prefix, latent, own_up, hidden_in)
    return pl.pallas_call(
        functools.partial(output_kernel, per_student),
        out_shape=(
            jax.ShapeDtypeStruct((tokens, width), BF16),
            jax.ShapeDtypeStruct((depth, ranks), F32),
            jax.ShapeDtypeStruct((ranks, width), F32),
        ),
        in_specs=[smem()] + [vmem()] * 3,
        out_specs=(vmem(), vmem(), vmem()),
        scratch_shapes=[
            pltpu.VMEM((2, ranks, depth), BF16),
            pltpu.VMEM((ranks, width), BF16),
        ],
        name="outputs",
    )(adapter_ids, att, grad, raised)


def solution(mesh):
    in_specs = (
        P("row", None),
        P("row", None),
        P("pre", None),
        P("pre", None),
        P(None, "pre"),
        P(),
        P("row", None),
        P(),
        P("row", None),
    )
    out_specs = (P("row", None), P("row", None), P())
    body = functools.partial(shards, mesh.shape["pre"], mesh.shape["row"])
    return jax.shard_map(body, mesh=mesh, in_specs=in_specs, out_specs=out_specs, check_vma=False)
```

```python
import functools
import math

import jax
import jax.numpy as jnp
from jax import lax
from jax.experimental import pallas as pl
from jax.experimental.pallas import tpu as pltpu
from jax.sharding import PartitionSpec as P

HD = 128
RANK = 16
MB = 128
ADAPTER_SCALE = 2.0
DEAD = -1e30
FLOOR = -1e29
TINY = 1e-30
STEP = 512
LOG2E = math.log2(math.e)
MESH = pl.DeviceIdType.MESH
F32 = jnp.float32
BF16 = jnp.bfloat16


def dot(a, b, ca, cb):
    return lax.dot_general(a, b, (((ca,), (cb,)), ((), ())), preferred_element_type=F32)


def remote(src, dst, send_sem, recv_sem, pre, row):
    return pltpu.make_async_remote_copy(
        src_ref=src,
        dst_ref=dst,
        send_sem=send_sem,
        recv_sem=recv_sem,
        device_id=(pre, row),
        device_id_type=MESH,
    )


def plane_offsets(row_count):
    extent = (4, 4, 2) if row_count == 32 else (1, row_count // 2, 2)
    around = lambda n, size: min(n, size - n)
    offsets = [
        (around(x, extent[0]) + around(y, extent[1]), x, y, c)
        for x in range(extent[0])
        for y in range(extent[1])
        for c in range(extent[2])
    ]
    return extent, [o[1:] for o in sorted(offsets, key=lambda o: -o[0]) if o[1:] != (0, 0, 0)]


def plane_peer(row, extent, offset):
    _, ys, cs = extent
    x = (row // (ys * cs) + offset[0]) % extent[0]
    y = (row // cs % ys + offset[1]) % ys
    return (x * ys + y) * cs + (row % cs + offset[2]) % cs


def line_offsets(count):
    return sorted(range(1, count), key=lambda k: -min(k, count - k))


def picker(ids_ref, students, ranks):
    place = lax.broadcasted_iota(jnp.int32, (ranks, ranks), 0)
    column = lax.broadcasted_iota(jnp.int32, (ranks, ranks), 1)
    wanted = jnp.zeros((ranks, ranks), jnp.int32)
    for s in range(students):
        wanted = jnp.where(place // RANK == s, ids_ref[s] * RANK + place % RANK, wanted)
    return jnp.where(column == wanted, 1.0, 0.0).astype(BF16)


def query_kernel(
    per_student,
    row_count,
    ids_ref,
    a_hbm,
    hidden_hbm,
    up_hbm,
    base_hbm,
    latent_ref,
    query_ref,
    own_up_ref,
    outgoing,
    incoming,
    a_rows,
    hidden,
    up_rows,
    base_rows,
    send_sem,
    recv_sem,
    load_sem,
):
    pre = lax.axis_index("pre")
    row = lax.axis_index("row")
    students = row_count // per_student
    depth, ranks = a_hbm.shape
    barrier = pltpu.get_barrier_semaphore()

    def greet(k, carry):
        pl.semaphore_signal(
            barrier, inc=1, device_id=(pre, (row + k) % row_count), device_id_type=MESH
        )
        return carry

    lax.fori_loop(1, row_count, greet, 0)
    loads = [
        pltpu.make_async_copy(source, landing, load_sem.at[n])
        for n, (source, landing) in enumerate(
            ((a_hbm, a_rows), (hidden_hbm, hidden), (up_hbm, up_rows), (base_hbm, base_rows))
        )
    ]
    for copy in loads:
        copy.start()
    pick = picker(ids_ref, students, ranks)
    loads[0].wait()
    picked = dot(pick, a_rows[...], 1, 1).astype(BF16)
    for s in range(students):
        outgoing[s] = picked[s * RANK : (s + 1) * RANK]
    pl.semaphore_wait(barrier, row_count - 1)

    extent, offsets = plane_offsets(row_count)
    own_cols = pl.ds(pl.multiple_of(row * depth, depth), depth)
    copies = []
    for k, offset in enumerate(offsets):
        to = plane_peer(row, extent, offset)
        copies.append(
            remote(
                outgoing.at[to // per_student],
                incoming.at[:, own_cols],
                send_sem.at[k],
                recv_sem.at[row],
                pre,
                to,
            )
        )
        copies[-1].start()
    mine = row // per_student
    incoming[:, own_cols] = outgoing[mine]
    place = lax.broadcasted_iota(jnp.int32, (RANK, ranks), 0)
    column = lax.broadcasted_iota(jnp.int32, (RANK, ranks), 1)
    own_pick = jnp.where(column == ids_ref[mine] * RANK + place, 1.0, 0.0).astype(BF16)
    for copy in loads[1:]:
        copy.wait()
    up = dot(own_pick, up_rows[...], 1, 0).astype(BF16)
    own_up_ref[...] = up

    def take(k, carry):
        source = (row + k) % row_count
        cols = pl.ds(pl.multiple_of(source * depth, depth), depth)
        remote(
            outgoing.at[0], incoming.at[:, cols], send_sem.at[0], recv_sem.at[source], pre, row
        ).wait_recv()
        return carry

    lax.fori_loop(1, row_count, take, 0)
    total = dot(incoming[...], hidden[...], 1, 1)
    latent = total.astype(BF16)
    latent_ref[...] = latent
    raised = dot(latent, up, 0, 0)
    query_ref[...] = (base_rows[...].astype(F32) + ADAPTER_SCALE * raised).astype(BF16)

    for copy in copies:
        copy.wait_send()


def split_parts(x, count):
    parts = []
    for _ in range(count):
        part = x.astype(BF16).astype(F32)
        parts.append(part)
        x = x - part
    return parts


def attention_kernel(
    pre_count,
    row_count,
    per_student,
    mask_ref,
    query_hbm,
    upstream_hbm,
    key_hbm,
    value_hbm,
    latent_ref,
    up_ref,
    hidden_hbm,
    attended_ref,
    grad_ref,
    raised_ref,
    hidden,
    q_rows,
    u_rows,
    bias,
    value_key,
    weights,
    high_rows,
    delta_rows,
    sum_rows,
    both_rows,
    back_rows,
    part,
    stat,
    stat_out,
    stat_in,
    sum_out,
    sum_in,
    term_out,
    term_in,
    att_in,
    quarter_out,
    quarter_in,
    lift_out,
    lift_in,
    grad_out,
    grad_in,
    up_out,
    up_in,
    raised,
    load_sem,
    input_sem,
    stat_send,
    stat_recv,
    sum_send,
    sum_recv,
    term_send,
    term_recv,
    att_send,
    att_recv,
    quarter_send,
    quarter_recv,
    lift_send,
    lift_recv,
    grad_send,
    grad_recv,
    up_send,
    up_recv,
):
    pre = lax.axis_index("pre")
    row = lax.axis_index("row")
    tokens = query_hbm.shape[0]
    heads = query_hbm.shape[1] // HD
    keys = key_hbm.shape[0]
    own_rows = heads * tokens // pre_count
    half = pre_count // 2
    stride = half // 2
    score_scale = 1.0 / math.sqrt(HD)
    fold = score_scale * LOG2E
    student = row // per_student
    place = row % per_student
    first_row = student * per_student
    depth = grad_out.shape[2]
    width = heads * HD // per_student
    extent, plane = plane_offsets(row_count)
    line = line_offsets(pre_count)
    barrier = pltpu.get_barrier_semaphore()

    loads = [
        pltpu.make_async_copy(key_hbm, value_key.at[:, HD:], input_sem.at[0]),
        pltpu.make_async_copy(value_hbm, value_key.at[:, :HD], input_sem.at[1]),
    ]
    for n, (source, landing) in enumerate(((query_hbm, q_rows), (upstream_hbm, u_rows))):
        for h in range(heads):
            loads.append(
                pltpu.make_async_copy(
                    source.at[:, h * HD : (h + 1) * HD],
                    landing.at[h * tokens : (h + 1) * tokens, :],
                    input_sem.at[2 + n * heads + h],
                )
            )
    for copy in loads:
        copy.start()
    load = pltpu.make_async_copy(hidden_hbm, hidden, load_sem)
    load.start()
    for k in line:
        pl.semaphore_signal(
            barrier, inc=1, device_id=((pre + k) % pre_count, row), device_id_type=MESH
        )
    for offset in plane:
        pl.semaphore_signal(
            barrier, inc=1, device_id=(pre, plane_peer(row, extent, offset)), device_id_type=MESH
        )

    for b in range(keys // MB):
        read = jnp.full((8, MB), mask_ref[student, b], jnp.int32)
        bias[:, b * MB : (b + 1) * MB] = jnp.where(read > 0, 0.0, DEAD)
    rows_all = heads * tokens
    step = weights.shape[2]
    lane = lax.broadcasted_iota(jnp.int32, (tokens, HD), 1)
    high_rows[...] = jnp.full((rows_all, HD), FLOOR, F32)
    for copy in loads:
        copy.wait()

    def score(j, carry):
        cols = pl.ds(pl.multiple_of(j * step, step), step)
        s = dot(q_rows[...], value_key[cols, HD:], 1, 1) + bias[0:1, cols]
        weights[j] = s
        high = high_rows[...]
        for g in range(step // HD):
            high = jnp.maximum(high, s[:, g * HD : (g + 1) * HD])
        high_rows[...] = high
        return carry

    lax.fori_loop(0, keys // step, score, 0)
    top = jnp.max(high_rows[...], axis=1, keepdims=True) * fold
    high_rows[...] = jnp.broadcast_to(top, (rows_all, HD))
    sum_rows[...] = jnp.zeros((rows_all, HD), F32)
    both_rows[...] = jnp.zeros((rows_all, 2 * HD), F32)

    def weigh(j, carry):
        cols = pl.ds(pl.multiple_of(j * step, step), step)
        level = high_rows[...]
        sums = sum_rows[...]
        ws = []
        for g in range(step // HD):
            w = jnp.exp2(weights[j, :, g * HD : (g + 1) * HD] * fold - level)
            weights[j, :, g * HD : (g + 1) * HD] = w
            sums = sums + w
            ws.append(w.astype(BF16))
        sum_rows[...] = sums
        both_rows[...] += dot(jnp.concatenate(ws, axis=1), value_key[cols, :], 1, 0)
        return carry

    lax.fori_loop(0, keys // step, weigh, 0)
    table = jnp.zeros((tokens, HD), F32)
    for h in range(heads):
        rows = slice(h * tokens, (h + 1) * tokens)
        l = jnp.maximum(jnp.sum(sum_rows[rows, :], axis=1, keepdims=True), TINY)
        weighed = u_rows[rows, :].astype(F32) * both_rows[rows, :HD]
        d = jnp.sum(weighed, axis=1, keepdims=True) / l
        lse = high_rows[rows, :] + jnp.log(l) * LOG2E
        delta_rows[rows, :] = jnp.broadcast_to(d, (tokens, HD))
        table = jnp.where(lane == h, lse, table)
        table = jnp.where(lane == heads + h, d, table)
    stat[...] = table

    stat_out[...] = stat[...].T[: 2 * heads]
    stat_in[pre] = stat_out[...]
    pl.semaphore_wait(barrier, row_count - 1 + pre_count - 1)

    def line_copies(source, landing, send_sem, recv_sem):
        return [
            remote(
                source,
                landing.at[pre],
                send_sem.at[n],
                recv_sem.at[pre],
                (pre + k) % pre_count,
                row,
            )
            for n, k in enumerate(line)
        ]

    def take_line(source, landing, send_sem, recv_sem):
        for k in reversed(line):
            origin = (pre + k) % pre_count
            remote(
                source, landing.at[origin], send_sem.at[0], recv_sem.at[origin], pre, row
            ).wait_recv()

    stat_copies = line_copies(stat_out, stat_in, stat_send, stat_recv)
    for copy in stat_copies:
        copy.start()

    back_rows[...] = jnp.zeros((rows_all, HD), F32)

    def backward(j, carry):
        cols = pl.ds(pl.multiple_of(j * step, step), step)
        dp = dot(u_rows[...], value_key[cols, :HD], 1, 1)
        d = delta_rows[...]
        g = [
            (weights[j, :, n * HD : (n + 1) * HD] * (dp[:, n * HD : (n + 1) * HD] - d)).astype(BF16)
            for n in range(step // HD)
        ]
        back_rows[...] += dot(jnp.concatenate(g, axis=1), value_key[cols, HD:], 1, 0)
        return carry

    lax.fori_loop(0, keys // step, backward, 0)

    take_line(stat_out, stat_in, stat_send, stat_recv)
    top = stat_in[0, :heads]
    for n in range(1, pre_count):
        top = jnp.maximum(top, stat_in[n, :heads])
    mass = jnp.zeros((heads, tokens), F32)
    mean = jnp.zeros((heads, tokens), F32)
    for n in range(pre_count):
        share = jnp.exp2(stat_in[n, :heads] - top)
        mass = mass + share
        mean = mean + share * stat_in[n, heads:]
    stat[:heads, :] = top + jnp.log(mass) * LOG2E
    stat[heads : 2 * heads, :] = mean / mass
    table = stat[...].T
    for h in range(heads):
        rows = slice(h * tokens, (h + 1) * tokens)
        factor = jnp.exp2(high_rows[rows, :] - table[:, h : h + 1])
        high_rows[rows, :] = factor
        part[rows, :] = both_rows[rows, :HD] * factor

    def hop(flow, distance):
        return (pre + (distance if flow == 0 else pre_count - distance)) % pre_count

    def own_part(flow, distance):
        chunk = hop(flow, distance)
        return part[pl.ds(pl.multiple_of(chunk * own_rows, own_rows), own_rows), :]

    def sum_copy(flow, distance):
        return remote(
            sum_out.at[flow, distance],
            sum_in.at[flow, distance],
            sum_send.at[flow, distance],
            sum_recv.at[flow, distance],
            hop(flow, distance if distance <= stride else distance - stride),
            row,
        )

    def reach(flow):
        return half - 1 + flow

    sent = []

    def send_sum(flow, distance, total):
        sum_out[flow, distance] = total.astype(BF16)
        sent.append(sum_copy(flow, distance))
        sent[-1].start()

    def arrivals(flow, distances, total):
        for distance in distances:
            sum_copy(flow, distance).wait_recv()
            total = total + sum_in[flow, distance].astype(F32)
        return total

    for distance in range(half, stride, -1):
        for flow in (1, 0):
            if distance <= reach(flow):
                send_sum(flow, distance, own_part(flow, distance))
    for distance in range(stride - 1, 0, -1):
        for flow in (1, 0):
            send_sum(flow, distance, own_part(flow, distance))

    code = jnp.zeros((RANK, tokens), F32)
    for h in range(heads):
        rows = slice(h * tokens, (h + 1) * tokens)
        cols = slice(h * HD, (h + 1) * HD)
        shift = delta_rows[rows, :] - table[:, heads + h : heads + h + 1]
        grad_q = (back_rows[rows, :] + shift * both_rows[rows, HD:]) * (high_rows[rows, :] * score_scale)
        grad_q = grad_q.astype(BF16)
        code = code + dot(up_ref[:, cols], grad_q, 1, 1)
        raised[:, cols] = ADAPTER_SCALE * dot(latent_ref[...], grad_q, 1, 0)
    term_out[...] = (ADAPTER_SCALE * code).astype(BF16)
    term_copies = line_copies(term_out, term_in, term_send, term_recv)
    for copy in term_copies:
        copy.start()
    term_in[pre] = term_out[...]
    for n in range(per_student):
        quarter_out[n] = raised[:, n * width : (n + 1) * width].astype(BF16)

    def quarter_copy(k):
        to = (place + k) % per_student
        return remote(
            quarter_out.at[to],
            quarter_in.at[place],
            quarter_send.at[k],
            quarter_recv.at[place],
            pre,
            first_row + to,
        )

    for k in range(1, per_student):
        quarter_copy(k).start()
    quarter_in[place] = quarter_out[place]

    for k in range(1, per_student):
        origin = (place + k) % per_student
        remote(
            quarter_out.at[0],
            quarter_in.at[origin],
            quarter_send.at[0],
            quarter_recv.at[origin],
            pre,
            row,
        ).wait_recv()
    summed = jnp.zeros((RANK, width), F32)
    for n in range(per_student):
        summed = summed + quarter_in[n].astype(F32)
    lift_out[...] = summed.astype(BF16)
    for flow in (1, 0):
        beyond = range(stride + 1, reach(flow) + 1)
        send_sum(flow, stride, arrivals(flow, beyond, own_part(flow, stride)))
    lift_copies = line_copies(lift_out, lift_in, lift_send, lift_recv)
    for copy in lift_copies:
        copy.start()
    lift_in[pre] = lift_out[...]

    total = own_part(0, 0)
    for flow in (0, 1):
        total = arrivals(flow, range(1, stride + 1), total)
    att_in[pre] = total.astype(BF16)
    att_copies = []

    def give(slot, flow, distance):
        n = len(att_copies)
        att_copies.append(
            remote(
                att_in.at[slot],
                att_in.at[slot],
                att_send.at[n],
                att_recv.at[slot],
                hop(flow, distance),
                row,
            )
        )
        att_copies[-1].start()

    for distance in range(stride, 0, -1):
        for flow in (1, 0):
            give(pre, flow, distance)

    load.wait()
    take_line(term_out, term_in, term_send, term_recv)
    code = term_in[0].astype(F32)
    for n in range(1, pre_count):
        code = code + term_in[n].astype(F32)
    code = code.astype(BF16)
    grad_copies = []
    for n, offset in enumerate(plane):
        to = plane_peer(row, extent, offset)
        cols = pl.ds(pl.multiple_of(to * depth, depth), depth)
        grad_out[to] = dot(code, hidden[:, cols], 1, 0).astype(BF16)
        grad_copies.append(
            remote(grad_out.at[to], grad_in.at[row], grad_send.at[n], grad_recv.at[row], pre, to)
        )
        grad_copies[-1].start()
    cols = pl.ds(pl.multiple_of(row * depth, depth), depth)
    grad_in[row] = dot(code, hidden[:, cols], 1, 0).astype(BF16)

    take_line(lift_out, lift_in, lift_send, lift_recv)
    summed = lift_in[0].astype(F32)
    for n in range(1, pre_count):
        summed = summed + lift_in[n].astype(F32)
    up_out[...] = summed.astype(BF16)
    up_copies = []
    for n, offset in enumerate(plane):
        to = plane_peer(row, extent, offset)
        up_copies.append(
            remote(up_out, up_in.at[row], up_send.at[n], up_recv.at[row], pre, to)
        )
        up_copies[-1].start()
    up_in[row] = up_out[...]

    def slot_wait(landing, slot, send_sem, recv_sem):
        remote(
            landing.at[slot], landing.at[slot], send_sem.at[0], recv_sem.at[slot], pre, row
        ).wait_recv()

    for flow in (1, 0):
        behind = hop(1 - flow, stride)
        slot_wait(att_in, behind, att_send, att_recv)
        for distance in range(reach(flow) - stride, 0, -1):
            give(behind, flow, distance)

    def take_grad(k, carry):
        slot_wait(grad_in, (row + k) % row_count, grad_send, grad_recv)
        return carry

    lax.fori_loop(1, row_count, take_grad, 0)
    grad_ref[...] = grad_in[...]
    for k in range(1, pre_count):
        if k not in (stride, pre_count - stride):
            slot_wait(att_in, (pre + k) % pre_count, att_send, att_recv)
    attended_ref[...] = att_in[...]

    def take_up(k, carry):
        slot_wait(up_in, (row + k) % row_count, up_send, up_recv)
        return carry

    lax.fori_loop(1, row_count, take_up, 0)
    raised_ref[...] = up_in[...]

    for copy in stat_copies + sent + term_copies + lift_copies + att_copies + grad_copies + up_copies:
        copy.wait_send()
    for k in range(1, per_student):
        quarter_copy(k).wait_send()


def output_kernel(
    per_student, ids_ref, att_ref, grad_ref, raised_ref, attended_ref, grad_a_ref, grad_up_ref, rows, ups
):
    count, own_rows, _ = att_ref.shape
    tokens = attended_ref.shape[0]
    pieces = tokens // own_rows
    students = grad_ref.shape[0] // per_student
    width = raised_ref.shape[2]
    pick = picker(ids_ref, students, students * RANK)
    for s in range(students):
        block_sum = grad_ref[s * per_student].astype(F32)
        for n in range(1, per_student):
            block_sum = block_sum + grad_ref[s * per_student + n].astype(F32)
        for n, piece in enumerate(split_parts(block_sum, 2)):
            rows[n, s * RANK : (s + 1) * RANK, :] = piece.astype(BF16)
        for j in range(per_student):
            ups[s * RANK : (s + 1) * RANK, j * width : (j + 1) * width] = raised_ref[
                s * per_student + j
            ]
    grad_a_ref[...] = dot(rows[0], pick, 0, 0) + dot(rows[1], pick, 0, 0)
    grad_up_ref[...] = dot(pick, ups[...], 0, 0)
    for c in range(count):
        h, n = c // pieces, c % pieces
        attended_ref[n * own_rows : (n + 1) * own_rows, h * HD : (h + 1) * HD] = att_ref[c]


def vmem():
    return pl.BlockSpec(memory_space=pltpu.VMEM)


def smem():
    return pl.BlockSpec(memory_space=pltpu.SMEM)


def anywhere():
    return pl.BlockSpec(memory_space=pl.ANY)


def shards(
    pre_count,
    row_count,
    hidden_in,
    frozen_query_base,
    k_prefix,
    v_prefix,
    tree_mask,
    adapter_ids,
    a_down,
    up_weight_matrix,
    cotangent,
):
    tokens, width = frozen_query_base.shape
    model = hidden_in.shape[1]
    heads = width // HD
    keys = k_prefix.shape[0]
    depth, ranks = a_down.shape
    students = tree_mask.shape[0]
    per_student = row_count // students
    dma = pltpu.SemaphoreType.DMA
    latent, queries, own_up = pl.pallas_call(
        functools.partial(query_kernel, per_student, row_count),
        out_shape=(
            jax.ShapeDtypeStruct((RANK, tokens), BF16),
            jax.ShapeDtypeStruct((tokens, width), BF16),
            jax.ShapeDtypeStruct((RANK, width), BF16),
        ),
        in_specs=[smem()] + [anywhere()] * 4,
        out_specs=(vmem(), vmem(), vmem()),
        scratch_shapes=[
            pltpu.VMEM((students, RANK, depth), BF16),
            pltpu.VMEM((RANK, model), BF16),
            pltpu.VMEM((depth, ranks), BF16),
            pltpu.VMEM((tokens, model), BF16),
            pltpu.VMEM((ranks, width), BF16),
            pltpu.VMEM((tokens, width), BF16),
            dma((row_count,)),
            dma((row_count,)),
            dma((4,)),
        ],
        compiler_params=pltpu.CompilerParams(collective_id=0, has_side_effects=True),
        name="queries",
    )(adapter_ids, a_down, hidden_in, up_weight_matrix, frozen_query_base)

    rows = heads * tokens
    own_rows = rows // pre_count
    quarter = width // per_student
    ring = (2, pre_count // 2 + 1)
    att, grad, raised = pl.pallas_call(
        functools.partial(attention_kernel, pre_count, row_count, per_student),
        out_shape=(
            jax.ShapeDtypeStruct((pre_count, own_rows, HD), BF16),
            jax.ShapeDtypeStruct((row_count, RANK, depth), BF16),
            jax.ShapeDtypeStruct((row_count, RANK, quarter), BF16),
        ),
        in_specs=[smem()] + [anywhere()] * 4 + [vmem()] * 2 + [anywhere()],
        out_specs=(vmem(), vmem(), vmem()),
        scratch_shapes=[
            pltpu.VMEM((tokens, model), BF16),
            pltpu.VMEM((rows, HD), BF16),
            pltpu.VMEM((rows, HD), BF16),
            pltpu.VMEM((8, keys), F32),
            pltpu.VMEM((keys, 2 * HD), BF16),
            pltpu.VMEM((keys // STEP, rows, STEP), F32),
            pltpu.VMEM((rows, HD), F32),
            pltpu.VMEM((rows, HD), F32),
            pltpu.VMEM((rows, HD), F32),
            pltpu.VMEM((rows, 2 * HD), F32),
            pltpu.VMEM((rows, HD), F32),
            pltpu.VMEM((rows, HD), F32),
            pltpu.VMEM((tokens, HD), F32),
            pltpu.VMEM((2 * heads, tokens), F32),
            pltpu.VMEM((pre_count, 2 * heads, tokens), F32),
            pltpu.VMEM(ring + (own_rows, HD), BF16),
            pltpu.VMEM(ring + (own_rows, HD), BF16),
            pltpu.VMEM((RANK, tokens), BF16),
            pltpu.VMEM((pre_count, RANK, tokens), BF16),
            pltpu.VMEM((pre_count, own_rows, HD), BF16),
            pltpu.VMEM((per_student, RANK, quarter), BF16),
            pltpu.VMEM((per_student, RANK, quarter), BF16),
            pltpu.VMEM((RANK, quarter), BF16),
            pltpu.VMEM((pre_count, RANK, quarter), BF16),
            pltpu.VMEM((row_count, RANK, depth), BF16),
            pltpu.VMEM((row_count, RANK, depth), BF16),
            pltpu.VMEM((RANK, quarter), BF16),
            pltpu.VMEM((row_count, RANK, quarter), BF16),
            pltpu.VMEM((RANK, width), F32),
            dma,
            dma((2 + 2 * heads,)),
            dma((pre_count,)),
            dma((pre_count,)),
            dma(ring),
            dma(ring),
            dma((pre_count,)),
            dma((pre_count,)),
            dma((pre_count,)),
            dma((pre_count,)),
            dma((per_student,)),
            dma((per_student,)),
            dma((pre_count,)),
            dma((pre_count,)),
            dma((row_count,)),
            dma((row_count,)),
            dma((row_count,)),
            dma((row_count,)),
        ],
        compiler_params=pltpu.CompilerParams(collective_id=1, has_side_effects=True),
        name="attention",
    )(tree_mask, queries, cotangent, k_prefix, v_prefix, latent, own_up, hidden_in)
    return pl.pallas_call(
        functools.partial(output_kernel, per_student),
        out_shape=(
            jax.ShapeDtypeStruct((tokens, width), BF16),
            jax.ShapeDtypeStruct((depth, ranks), F32),
            jax.ShapeDtypeStruct((ranks, width), F32),
        ),
        in_specs=[smem()] + [vmem()] * 3,
        out_specs=(vmem(), vmem(), vmem()),
        scratch_shapes=[
            pltpu.VMEM((2, ranks, depth), BF16),
            pltpu.VMEM((ranks, width), BF16),
        ],
        name="outputs",
    )(adapter_ids, att, grad, raised)


def solution(mesh):
    in_specs = (
        P("row", None),
        P("row", None),
        P("pre", None),
        P("pre", None),
        P(None, "pre"),
        P(),
        P("row", None),
        P(),
        P("row", None),
    )
    out_specs = (P("row", None), P("row", None), P())
    body = functools.partial(shards, mesh.shape["pre"], mesh.shape["row"])
    return jax.shard_map(body, mesh=mesh, in_specs=in_specs, out_specs=out_specs, check_vma=False)
```

```python
import functools
import math

import jax
import jax.numpy as jnp
from jax import lax
from jax.experimental import pallas as pl
from jax.experimental.pallas import tpu as pltpu
from jax.sharding import PartitionSpec as P

HD = 128
RANK = 16
MB = 128
ADAPTER_SCALE = 2.0
DEAD = -1e30
FLOOR = -1e29
TINY = 1e-30
STEP = 1024
LOG2E = math.log2(math.e)
MESH = pl.DeviceIdType.MESH
F32 = jnp.float32
BF16 = jnp.bfloat16


def dot(a, b, ca, cb):
    return lax.dot_general(a, b, (((ca,), (cb,)), ((), ())), preferred_element_type=F32)


def remote(src, dst, send_sem, recv_sem, pre, row):
    return pltpu.make_async_remote_copy(
        src_ref=src,
        dst_ref=dst,
        send_sem=send_sem,
        recv_sem=recv_sem,
        device_id=(pre, row),
        device_id_type=MESH,
    )


def plane_offsets(row_count):
    extent = (4, 4, 2) if row_count == 32 else (1, row_count // 2, 2)
    around = lambda n, size: min(n, size - n)
    offsets = [
        (around(x, extent[0]) + around(y, extent[1]), x, y, c)
        for x in range(extent[0])
        for y in range(extent[1])
        for c in range(extent[2])
    ]
    return extent, [o[1:] for o in sorted(offsets, key=lambda o: -o[0]) if o[1:] != (0, 0, 0)]


def plane_peer(row, extent, offset):
    _, ys, cs = extent
    x = (row // (ys * cs) + offset[0]) % extent[0]
    y = (row // cs % ys + offset[1]) % ys
    return (x * ys + y) * cs + (row % cs + offset[2]) % cs


def line_offsets(count):
    return sorted(range(1, count), key=lambda k: -min(k, count - k))


def picker(ids_ref, students, ranks):
    place = lax.broadcasted_iota(jnp.int32, (ranks, ranks), 0)
    column = lax.broadcasted_iota(jnp.int32, (ranks, ranks), 1)
    wanted = jnp.zeros((ranks, ranks), jnp.int32)
    for s in range(students):
        wanted = jnp.where(place // RANK == s, ids_ref[s] * RANK + place % RANK, wanted)
    return jnp.where(column == wanted, 1.0, 0.0).astype(BF16)


def query_kernel(
    per_student,
    row_count,
    ids_ref,
    a_hbm,
    hidden_hbm,
    up_hbm,
    base_hbm,
    latent_ref,
    query_ref,
    own_up_ref,
    outgoing,
    incoming,
    a_rows,
    hidden,
    up_rows,
    base_rows,
    send_sem,
    recv_sem,
    load_sem,
):
    pre = lax.axis_index("pre")
    row = lax.axis_index("row")
    students = row_count // per_student
    depth, ranks = a_hbm.shape
    barrier = pltpu.get_barrier_semaphore()

    def greet(k, carry):
        pl.semaphore_signal(
            barrier, inc=1, device_id=(pre, (row + k) % row_count), device_id_type=MESH
        )
        return carry

    lax.fori_loop(1, row_count, greet, 0)
    loads = [
        pltpu.make_async_copy(source, landing, load_sem.at[n])
        for n, (source, landing) in enumerate(
            ((a_hbm, a_rows), (hidden_hbm, hidden), (up_hbm, up_rows), (base_hbm, base_rows))
        )
    ]
    for copy in loads:
        copy.start()
    pick = picker(ids_ref, students, ranks)
    loads[0].wait()
    picked = dot(pick, a_rows[...], 1, 1).astype(BF16)
    for s in range(students):
        outgoing[s] = picked[s * RANK : (s + 1) * RANK]
    pl.semaphore_wait(barrier, row_count - 1)

    extent, offsets = plane_offsets(row_count)
    own_cols = pl.ds(pl.multiple_of(row * depth, depth), depth)
    copies = []
    for k, offset in enumerate(offsets):
        to = plane_peer(row, extent, offset)
        copies.append(
            remote(
                outgoing.at[to // per_student],
                incoming.at[:, own_cols],
                send_sem.at[k],
                recv_sem.at[row],
                pre,
                to,
            )
        )
        copies[-1].start()
    mine = row // per_student
    incoming[:, own_cols] = outgoing[mine]
    place = lax.broadcasted_iota(jnp.int32, (RANK, ranks), 0)
    column = lax.broadcasted_iota(jnp.int32, (RANK, ranks), 1)
    own_pick = jnp.where(column == ids_ref[mine] * RANK + place, 1.0, 0.0).astype(BF16)
    for copy in loads[1:]:
        copy.wait()
    up = dot(own_pick, up_rows[...], 1, 0).astype(BF16)
    own_up_ref[...] = up

    def take(k, carry):
        source = (row + k) % row_count
        cols = pl.ds(pl.multiple_of(source * depth, depth), depth)
        remote(
            outgoing.at[0], incoming.at[:, cols], send_sem.at[0], recv_sem.at[source], pre, row
        ).wait_recv()
        return carry

    lax.fori_loop(1, row_count, take, 0)
    total = dot(incoming[...], hidden[...], 1, 1)
    latent = total.astype(BF16)
    latent_ref[...] = latent
    raised = dot(latent, up, 0, 0)
    query_ref[...] = (base_rows[...].astype(F32) + ADAPTER_SCALE * raised).astype(BF16)

    for copy in copies:
        copy.wait_send()


def split_parts(x, count):
    parts = []
    for _ in range(count):
        part = x.astype(BF16).astype(F32)
        parts.append(part)
        x = x - part
    return parts


def attention_kernel(
    pre_count,
    row_count,
    per_student,
    mask_ref,
    query_hbm,
    upstream_hbm,
    key_hbm,
    value_hbm,
    latent_ref,
    up_ref,
    hidden_hbm,
    attended_ref,
    grad_ref,
    raised_ref,
    hidden,
    q_rows,
    u_rows,
    bias,
    value_key,
    weights,
    high_rows,
    delta_rows,
    sum_rows,
    both_rows,
    back_rows,
    part,
    stat,
    stat_out,
    stat_in,
    sum_out,
    sum_in,
    term_out,
    term_in,
    att_in,
    quarter_out,
    quarter_in,
    lift_out,
    lift_in,
    grad_out,
    grad_in,
    up_out,
    up_in,
    raised,
    load_sem,
    input_sem,
    stat_send,
    stat_recv,
    sum_send,
    sum_recv,
    term_send,
    term_recv,
    att_send,
    att_recv,
    quarter_send,
    quarter_recv,
    lift_send,
    lift_recv,
    grad_send,
    grad_recv,
    up_send,
    up_recv,
):
    pre = lax.axis_index("pre")
    row = lax.axis_index("row")
    tokens = query_hbm.shape[0]
    heads = query_hbm.shape[1] // HD
    keys = key_hbm.shape[0]
    own_rows = heads * tokens // pre_count
    half = pre_count // 2
    stride = half // 2
    score_scale = 1.0 / math.sqrt(HD)
    fold = score_scale * LOG2E
    student = row // per_student
    place = row % per_student
    first_row = student * per_student
    depth = grad_out.shape[2]
    width = heads * HD // per_student
    extent, plane = plane_offsets(row_count)
    line = line_offsets(pre_count)
    barrier = pltpu.get_barrier_semaphore()

    loads = [
        pltpu.make_async_copy(key_hbm, value_key.at[:, HD:], input_sem.at[0]),
        pltpu.make_async_copy(value_hbm, value_key.at[:, :HD], input_sem.at[1]),
    ]
    for n, (source, landing) in enumerate(((query_hbm, q_rows), (upstream_hbm, u_rows))):
        for h in range(heads):
            loads.append(
                pltpu.make_async_copy(
                    source.at[:, h * HD : (h + 1) * HD],
                    landing.at[h * tokens : (h + 1) * tokens, :],
                    input_sem.at[2 + n * heads + h],
                )
            )
    for copy in loads:
        copy.start()
    load = pltpu.make_async_copy(hidden_hbm, hidden, load_sem)
    load.start()
    for k in line:
        pl.semaphore_signal(
            barrier, inc=1, device_id=((pre + k) % pre_count, row), device_id_type=MESH
        )
    for offset in plane:
        pl.semaphore_signal(
            barrier, inc=1, device_id=(pre, plane_peer(row, extent, offset)), device_id_type=MESH
        )

    for b in range(keys // MB):
        read = jnp.full((8, MB), mask_ref[student, b], jnp.int32)
        bias[:, b * MB : (b + 1) * MB] = jnp.where(read > 0, 0.0, DEAD)
    rows_all = heads * tokens
    step = weights.shape[2]
    lane = lax.broadcasted_iota(jnp.int32, (tokens, HD), 1)
    high_rows[...] = jnp.full((rows_all, HD), FLOOR, F32)
    for copy in loads:
        copy.wait()

    def score(j, carry):
        cols = pl.ds(pl.multiple_of(j * step, step), step)
        s = dot(q_rows[...], value_key[cols, HD:], 1, 1) + bias[0:1, cols]
        weights[j] = s
        high = high_rows[...]
        for g in range(step // HD):
            high = jnp.maximum(high, s[:, g * HD : (g + 1) * HD])
        high_rows[...] = high
        return carry

    lax.fori_loop(0, keys // step, score, 0)
    top = jnp.max(high_rows[...], axis=1, keepdims=True) * fold
    high_rows[...] = jnp.broadcast_to(top, (rows_all, HD))
    sum_rows[...] = jnp.zeros((rows_all, HD), F32)
    both_rows[...] = jnp.zeros((rows_all, 2 * HD), F32)

    def weigh(j, carry):
        cols = pl.ds(pl.multiple_of(j * step, step), step)
        level = high_rows[...]
        sums = sum_rows[...]
        ws = []
        for g in range(step // HD):
            w = jnp.exp2(weights[j, :, g * HD : (g + 1) * HD] * fold - level)
            weights[j, :, g * HD : (g + 1) * HD] = w
            sums = sums + w
            ws.append(w.astype(BF16))
        sum_rows[...] = sums
        both_rows[...] += dot(jnp.concatenate(ws, axis=1), value_key[cols, :], 1, 0)
        return carry

    lax.fori_loop(0, keys // step, weigh, 0)
    table = jnp.zeros((tokens, HD), F32)
    for h in range(heads):
        rows = slice(h * tokens, (h + 1) * tokens)
        l = jnp.maximum(jnp.sum(sum_rows[rows, :], axis=1, keepdims=True), TINY)
        weighed = u_rows[rows, :].astype(F32) * both_rows[rows, :HD]
        d = jnp.sum(weighed, axis=1, keepdims=True) / l
        lse = high_rows[rows, :] + jnp.log(l) * LOG2E
        delta_rows[rows, :] = jnp.broadcast_to(d, (tokens, HD))
        table = jnp.where(lane == h, lse, table)
        table = jnp.where(lane == heads + h, d, table)
    stat[...] = table

    stat_out[...] = stat[...].T[: 2 * heads]
    stat_in[pre] = stat_out[...]
    pl.semaphore_wait(barrier, row_count - 1 + pre_count - 1)

    def line_copies(source, landing, send_sem, recv_sem):
        return [
            remote(
                source,
                landing.at[pre],
                send_sem.at[n],
                recv_sem.at[pre],
                (pre + k) % pre_count,
                row,
            )
            for n, k in enumerate(line)
        ]

    def take_line(source, landing, send_sem, recv_sem):
        for k in reversed(line):
            origin = (pre + k) % pre_count
            remote(
                source, landing.at[origin], send_sem.at[0], recv_sem.at[origin], pre, row
            ).wait_recv()

    stat_copies = line_copies(stat_out, stat_in, stat_send, stat_recv)
    for copy in stat_copies:
        copy.start()

    back_rows[...] = jnp.zeros((rows_all, HD), F32)

    def backward(j, carry):
        cols = pl.ds(pl.multiple_of(j * step, step), step)
        dp = dot(u_rows[...], value_key[cols, :HD], 1, 1)
        d = delta_rows[...]
        g = [
            (weights[j, :, n * HD : (n + 1) * HD] * (dp[:, n * HD : (n + 1) * HD] - d)).astype(BF16)
            for n in range(step // HD)
        ]
        back_rows[...] += dot(jnp.concatenate(g, axis=1), value_key[cols, HD:], 1, 0)
        return carry

    lax.fori_loop(0, keys // step, backward, 0)

    take_line(stat_out, stat_in, stat_send, stat_recv)
    top = stat_in[0, :heads]
    for n in range(1, pre_count):
        top = jnp.maximum(top, stat_in[n, :heads])
    mass = jnp.zeros((heads, tokens), F32)
    mean = jnp.zeros((heads, tokens), F32)
    for n in range(pre_count):
        share = jnp.exp2(stat_in[n, :heads] - top)
        mass = mass + share
        mean = mean + share * stat_in[n, heads:]
    stat[:heads, :] = top + jnp.log(mass) * LOG2E
    stat[heads : 2 * heads, :] = mean / mass
    table = stat[...].T
    for h in range(heads):
        rows = slice(h * tokens, (h + 1) * tokens)
        factor = jnp.exp2(high_rows[rows, :] - table[:, h : h + 1])
        high_rows[rows, :] = factor
        part[rows, :] = both_rows[rows, :HD] * factor

    def hop(flow, distance):
        return (pre + (distance if flow == 0 else pre_count - distance)) % pre_count

    def own_part(flow, distance):
        chunk = hop(flow, distance)
        return part[pl.ds(pl.multiple_of(chunk * own_rows, own_rows), own_rows), :]

    def sum_copy(flow, distance):
        return remote(
            sum_out.at[flow, distance],
            sum_in.at[flow, distance],
            sum_send.at[flow, distance],
            sum_recv.at[flow, distance],
            hop(flow, distance if distance <= stride else distance - stride),
            row,
        )

    def reach(flow):
        return half - 1 + flow

    sent = []

    def send_sum(flow, distance, total):
        sum_out[flow, distance] = total.astype(BF16)
        sent.append(sum_copy(flow, distance))
        sent[-1].start()

    def arrivals(flow, distances, total):
        for distance in distances:
            sum_copy(flow, distance).wait_recv()
            total = total + sum_in[flow, distance].astype(F32)
        return total

    for distance in range(half, stride, -1):
        for flow in (1, 0):
            if distance <= reach(flow):
                send_sum(flow, distance, own_part(flow, distance))
    for distance in range(stride - 1, 0, -1):
        for flow in (1, 0):
            send_sum(flow, distance, own_part(flow, distance))

    code = jnp.zeros((RANK, tokens), F32)
    for h in range(heads):
        rows = slice(h * tokens, (h + 1) * tokens)
        cols = slice(h * HD, (h + 1) * HD)
        shift = delta_rows[rows, :] - table[:, heads + h : heads + h + 1]
        grad_q = (back_rows[rows, :] + shift * both_rows[rows, HD:]) * (high_rows[rows, :] * score_scale)
        grad_q = grad_q.astype(BF16)
        code = code + dot(up_ref[:, cols], grad_q, 1, 1)
        raised[:, cols] = ADAPTER_SCALE * dot(latent_ref[...], grad_q, 1, 0)
    term_out[...] = (ADAPTER_SCALE * code).astype(BF16)
    term_copies = line_copies(term_out, term_in, term_send, term_recv)
    for copy in term_copies:
        copy.start()
    term_in[pre] = term_out[...]
    for n in range(per_student):
        quarter_out[n] = raised[:, n * width : (n + 1) * width].astype(BF16)

    def quarter_copy(k):
        to = (place + k) % per_student
        return remote(
            quarter_out.at[to],
            quarter_in.at[place],
            quarter_send.at[k],
            quarter_recv.at[place],
            pre,
            first_row + to,
        )

    for k in range(1, per_student):
        quarter_copy(k).start()
    quarter_in[place] = quarter_out[place]

    for k in range(1, per_student):
        origin = (place + k) % per_student
        remote(
            quarter_out.at[0],
            quarter_in.at[origin],
            quarter_send.at[0],
            quarter_recv.at[origin],
            pre,
            row,
        ).wait_recv()
    summed = jnp.zeros((RANK, width), F32)
    for n in range(per_student):
        summed = summed + quarter_in[n].astype(F32)
    lift_out[...] = summed.astype(BF16)
    for flow in (1, 0):
        beyond = range(stride + 1, reach(flow) + 1)
        send_sum(flow, stride, arrivals(flow, beyond, own_part(flow, stride)))
    lift_copies = line_copies(lift_out, lift_in, lift_send, lift_recv)
    for copy in lift_copies:
        copy.start()
    lift_in[pre] = lift_out[...]

    total = own_part(0, 0)
    for flow in (0, 1):
        total = arrivals(flow, range(1, stride + 1), total)
    att_in[pre] = total.astype(BF16)
    att_copies = []

    def give(slot, flow, distance):
        n = len(att_copies)
        att_copies.append(
            remote(
                att_in.at[slot],
                att_in.at[slot],
                att_send.at[n],
                att_recv.at[slot],
                hop(flow, distance),
                row,
            )
        )
        att_copies[-1].start()

    for distance in range(stride, 0, -1):
        for flow in (1, 0):
            give(pre, flow, distance)

    load.wait()
    take_line(term_out, term_in, term_send, term_recv)
    code = term_in[0].astype(F32)
    for n in range(1, pre_count):
        code = code + term_in[n].astype(F32)
    code = code.astype(BF16)
    grad_copies = []
    for n, offset in enumerate(plane):
        to = plane_peer(row, extent, offset)
        cols = pl.ds(pl.multiple_of(to * depth, depth), depth)
        grad_out[to] = dot(code, hidden[:, cols], 1, 0).astype(BF16)
        grad_copies.append(
            remote(grad_out.at[to], grad_in.at[row], grad_send.at[n], grad_recv.at[row], pre, to)
        )
        grad_copies[-1].start()
    cols = pl.ds(pl.multiple_of(row * depth, depth), depth)
    grad_in[row] = dot(code, hidden[:, cols], 1, 0).astype(BF16)

    take_line(lift_out, lift_in, lift_send, lift_recv)
    summed = lift_in[0].astype(F32)
    for n in range(1, pre_count):
        summed = summed + lift_in[n].astype(F32)
    up_out[...] = summed.astype(BF16)
    up_copies = []
    for n, offset in enumerate(plane):
        to = plane_peer(row, extent, offset)
        up_copies.append(
            remote(up_out, up_in.at[row], up_send.at[n], up_recv.at[row], pre, to)
        )
        up_copies[-1].start()
    up_in[row] = up_out[...]

    def slot_wait(landing, slot, send_sem, recv_sem):
        remote(
            landing.at[slot], landing.at[slot], send_sem.at[0], recv_sem.at[slot], pre, row
        ).wait_recv()

    for flow in (1, 0):
        behind = hop(1 - flow, stride)
        slot_wait(att_in, behind, att_send, att_recv)
        for distance in range(reach(flow) - stride, 0, -1):
            give(behind, flow, distance)

    def take_grad(k, carry):
        slot_wait(grad_in, (row + k) % row_count, grad_send, grad_recv)
        return carry

    lax.fori_loop(1, row_count, take_grad, 0)
    grad_ref[...] = grad_in[...]
    for k in range(1, pre_count):
        if k not in (stride, pre_count - stride):
            slot_wait(att_in, (pre + k) % pre_count, att_send, att_recv)
    attended_ref[...] = att_in[...]

    def take_up(k, carry):
        slot_wait(up_in, (row + k) % row_count, up_send, up_recv)
        return carry

    lax.fori_loop(1, row_count, take_up, 0)
    raised_ref[...] = up_in[...]

    for copy in stat_copies + sent + term_copies + lift_copies + att_copies + grad_copies + up_copies:
        copy.wait_send()
    for k in range(1, per_student):
        quarter_copy(k).wait_send()


def output_kernel(
    per_student, ids_ref, att_ref, grad_ref, raised_ref, attended_ref, grad_a_ref, grad_up_ref, rows, ups
):
    count, own_rows, _ = att_ref.shape
    tokens = attended_ref.shape[0]
    pieces = tokens // own_rows
    students = grad_ref.shape[0] // per_student
    width = raised_ref.shape[2]
    pick = picker(ids_ref, students, students * RANK)
    for s in range(students):
        block_sum = grad_ref[s * per_student].astype(F32)
        for n in range(1, per_student):
            block_sum = block_sum + grad_ref[s * per_student + n].astype(F32)
        for n, piece in enumerate(split_parts(block_sum, 2)):
            rows[n, s * RANK : (s + 1) * RANK, :] = piece.astype(BF16)
        for j in range(per_student):
            ups[s * RANK : (s + 1) * RANK, j * width : (j + 1) * width] = raised_ref[
                s * per_student + j
            ]
    grad_a_ref[...] = dot(rows[0], pick, 0, 0) + dot(rows[1], pick, 0, 0)
    grad_up_ref[...] = dot(pick, ups[...], 0, 0)
    for c in range(count):
        h, n = c // pieces, c % pieces
        attended_ref[n * own_rows : (n + 1) * own_rows, h * HD : (h + 1) * HD] = att_ref[c]


def vmem():
    return pl.BlockSpec(memory_space=pltpu.VMEM)


def smem():
    return pl.BlockSpec(memory_space=pltpu.SMEM)


def anywhere():
    return pl.BlockSpec(memory_space=pl.ANY)


def shards(
    pre_count,
    row_count,
    hidden_in,
    frozen_query_base,
    k_prefix,
    v_prefix,
    tree_mask,
    adapter_ids,
    a_down,
    up_weight_matrix,
    cotangent,
):
    tokens, width = frozen_query_base.shape
    model = hidden_in.shape[1]
    heads = width // HD
    keys = k_prefix.shape[0]
    depth, ranks = a_down.shape
    students = tree_mask.shape[0]
    per_student = row_count // students
    dma = pltpu.SemaphoreType.DMA
    latent, queries, own_up = pl.pallas_call(
        functools.partial(query_kernel, per_student, row_count),
        out_shape=(
            jax.ShapeDtypeStruct((RANK, tokens), BF16),
            jax.ShapeDtypeStruct((tokens, width), BF16),
            jax.ShapeDtypeStruct((RANK, width), BF16),
        ),
        in_specs=[smem()] + [anywhere()] * 4,
        out_specs=(vmem(), vmem(), vmem()),
        scratch_shapes=[
            pltpu.VMEM((students, RANK, depth), BF16),
            pltpu.VMEM((RANK, model), BF16),
            pltpu.VMEM((depth, ranks), BF16),
            pltpu.VMEM((tokens, model), BF16),
            pltpu.VMEM((ranks, width), BF16),
            pltpu.VMEM((tokens, width), BF16),
            dma((row_count,)),
            dma((row_count,)),
            dma((4,)),
        ],
        compiler_params=pltpu.CompilerParams(collective_id=0, has_side_effects=True),
        name="queries",
    )(adapter_ids, a_down, hidden_in, up_weight_matrix, frozen_query_base)

    rows = heads * tokens
    own_rows = rows // pre_count
    quarter = width // per_student
    ring = (2, pre_count // 2 + 1)
    att, grad, raised = pl.pallas_call(
        functools.partial(attention_kernel, pre_count, row_count, per_student),
        out_shape=(
            jax.ShapeDtypeStruct((pre_count, own_rows, HD), BF16),
            jax.ShapeDtypeStruct((row_count, RANK, depth), BF16),
            jax.ShapeDtypeStruct((row_count, RANK, quarter), BF16),
        ),
        in_specs=[smem()] + [anywhere()] * 4 + [vmem()] * 2 + [anywhere()],
        out_specs=(vmem(), vmem(), vmem()),
        scratch_shapes=[
            pltpu.VMEM((tokens, model), BF16),
            pltpu.VMEM((rows, HD), BF16),
            pltpu.VMEM((rows, HD), BF16),
            pltpu.VMEM((8, keys), F32),
            pltpu.VMEM((keys, 2 * HD), BF16),
            pltpu.VMEM((keys // STEP, rows, STEP), F32),
            pltpu.VMEM((rows, HD), F32),
            pltpu.VMEM((rows, HD), F32),
            pltpu.VMEM((rows, HD), F32),
            pltpu.VMEM((rows, 2 * HD), F32),
            pltpu.VMEM((rows, HD), F32),
            pltpu.VMEM((rows, HD), F32),
            pltpu.VMEM((tokens, HD), F32),
            pltpu.VMEM((2 * heads, tokens), F32),
            pltpu.VMEM((pre_count, 2 * heads, tokens), F32),
            pltpu.VMEM(ring + (own_rows, HD), BF16),
            pltpu.VMEM(ring + (own_rows, HD), BF16),
            pltpu.VMEM((RANK, tokens), BF16),
            pltpu.VMEM((pre_count, RANK, tokens), BF16),
            pltpu.VMEM((pre_count, own_rows, HD), BF16),
            pltpu.VMEM((per_student, RANK, quarter), BF16),
            pltpu.VMEM((per_student, RANK, quarter), BF16),
            pltpu.VMEM((RANK, quarter), BF16),
            pltpu.VMEM((pre_count, RANK, quarter), BF16),
            pltpu.VMEM((row_count, RANK, depth), BF16),
            pltpu.VMEM((row_count, RANK, depth), BF16),
            pltpu.VMEM((RANK, quarter), BF16),
            pltpu.VMEM((row_count, RANK, quarter), BF16),
            pltpu.VMEM((RANK, width), F32),
            dma,
            dma((2 + 2 * heads,)),
            dma((pre_count,)),
            dma((pre_count,)),
            dma(ring),
            dma(ring),
            dma((pre_count,)),
            dma((pre_count,)),
            dma((pre_count,)),
            dma((pre_count,)),
            dma((per_student,)),
            dma((per_student,)),
            dma((pre_count,)),
            dma((pre_count,)),
            dma((row_count,)),
            dma((row_count,)),
            dma((row_count,)),
            dma((row_count,)),
        ],
        compiler_params=pltpu.CompilerParams(collective_id=1, has_side_effects=True),
        name="attention",
    )(tree_mask, queries, cotangent, k_prefix, v_prefix, latent, own_up, hidden_in)
    return pl.pallas_call(
        functools.partial(output_kernel, per_student),
        out_shape=(
            jax.ShapeDtypeStruct((tokens, width), BF16),
            jax.ShapeDtypeStruct((depth, ranks), F32),
            jax.ShapeDtypeStruct((ranks, width), F32),
        ),
        in_specs=[smem()] + [vmem()] * 3,
        out_specs=(vmem(), vmem(), vmem()),
        scratch_shapes=[
            pltpu.VMEM((2, ranks, depth), BF16),
            pltpu.VMEM((ranks, width), BF16),
        ],
        name="outputs",
    )(adapter_ids, att, grad, raised)


def solution(mesh):
    in_specs = (
        P("row", None),
        P("row", None),
        P("pre", None),
        P("pre", None),
        P(None, "pre"),
        P(),
        P("row", None),
        P(),
        P("row", None),
    )
    out_specs = (P("row", None), P("row", None), P())
    body = functools.partial(shards, mesh.shape["pre"], mesh.shape["row"])
    return jax.shard_map(body, mesh=mesh, in_specs=in_specs, out_specs=out_specs, check_vma=False)
```
